256 devices in a mesh: seq: 32 (over y, z), ch: 8 (over x, core).
Axes of the slice: x: 4, y: 4, z: 8, core: 2. Of those that a mesh axis runs over, the one named last changes fastest.
Arguments:
- genome: int32 [8192, 128], P('seq'), may hold values from 0 to 3
- stem_weight: bfloat16 [768, 512], P('ch'), may hold values from -0.5 to 0.5
- dilated_filter_weight: bfloat16 [5, 3, 768, 768], P(None, None, 'ch'), may hold values from -0.125 to 0.125
- head_weight: bfloat16 [768, 5313], P('ch'), may hold values from -0.21875 to 0.21875
- window_start: int32 [512], replicated, may hold values from 0 to 8176
- window_track: int32 [512], replicated, may hold values from 0 to 5312
- targets: float32 [512], replicated, may hold values from 0 to 3
Outputs:
- window_score: float32 [512], replicated
- conv_grad: float32 [5, 3, 768, 768], P(None, None, 'ch', 'seq')
- stem_grad: float32 [768, 512], P('ch')
- head_grad: float32 [768, 5313], P('ch')
The draws below stay inside these ranges and needn't reach their ends.
Inputs may be any that keep to these rules, and one draw needn't show every extreme that they name: `window_start`: each window lies inside the sequence.
All inputs are finite; a program needn't handle non-finite values.
Results may differ from the reference program's by a relative error of at most 0.0037.
Values may be sent and summed in bfloat16 or wider, within the bound.
A program may use at most 128 MiB of HBM per device.

```python
import math
import jax
import jax.numpy as jnp
import numpy as np
from jax import lax

C = 768
TRACKS = 5313
POOL = 128
ROWS = 256
LAYERS = 5
WIN = 16
BINS = 8192
WINDOWS = 512


def touch_ends(values, own_key, low, top_value):
    spot = [jax.random.randint(jax.random.fold_in(own_key, axis), (), 0, length) for axis, length in enumerate(values.shape)]
    main_axis = values.shape.index(max(values.shape))
    next_to = spot[:main_axis] + [(spot[main_axis] + 1) % values.shape[main_axis]] + spot[main_axis + 1:]
    return values.at[tuple(spot)].set(low).at[tuple(next_to)].set(top_value)


def shard_levels(own_key, extent, cuts, smallest, top_value):
    level = 1.0
    for axis_at, shards_of in cuts:
        heights = jax.random.uniform(jax.random.fold_in(jax.random.fold_in(own_key, 6), axis_at), (shards_of,), jnp.float32, smallest / len(cuts), top_value / len(cuts))
        level = level * jnp.repeat(jnp.exp(heights), extent[axis_at] // shards_of).reshape((-1,) + (1,) * (len(extent) - 1 - axis_at))
    return level


def rank_bounds(number_of, skew):
    portions = [(1 << 20) // math.isqrt(grade ** skew) + 1 for grade in range(1, number_of + 1)]
    deviation = 1 + sum(portions) // (1 << 30)
    return np.cumsum(np.array([max(1, weight // deviation) for weight in portions]))


def ranked(rng, extent, count, skew):
    listing = rank_bounds(count, skew)
    ticket = jax.random.randint(jax.random.fold_in(rng, 1), extent, 0, int(listing[count - 1]))
    standing = jnp.searchsorted(jnp.asarray(listing, jnp.int32), ticket, side="right")
    return jax.random.permutation(jax.random.fold_in(rng, 2), count)[standing].astype(jnp.int32)


def gaussian(key, extent, width, most, shards=(), kind=jnp.bfloat16):
    array = width * jax.random.normal(key, extent, jnp.float32)
    if shards:
        array = array * shard_levels(key, extent, shards, -0.22, 0.18)
    return jnp.clip(array, -most, most).astype(kind)


def setup_inputs(seed: int = 0) -> dict:
    keys = jax.random.split(jax.random.key(seed), 8)
    genome = touch_ends(jax.random.randint(keys[0], (BINS, POOL), 0, 4), jax.random.fold_in(keys[0], 1), 0, 3).astype(jnp.int32)
    stem_weight = gaussian(keys[1], (C, 4 * POOL), POOL ** -0.5, 0.5, ((0, 8),))
    dilated_filter_weight = gaussian(keys[2], (LAYERS, 3, C, C), (3 * C) ** -0.5, 0.125, ((2, 8),))
    head_weight = gaussian(keys[3], (C, TRACKS), C ** -0.5, 0.21875, ((0, 8),))
    window_start = touch_ends(jax.random.randint(keys[4], (WINDOWS,), 0, BINS - WIN + 1), jax.random.fold_in(keys[4], 1), 0, BINS - WIN).astype(jnp.int32)
    window_track = touch_ends(ranked(keys[5], (WINDOWS,), TRACKS, 2), jax.random.fold_in(keys[5], 3), 0, TRACKS - 1).astype(jnp.int32)
    targets = jnp.clip(jax.random.uniform(keys[6], (WINDOWS,), jnp.float32, 0.0, 3.0), 0.0, 3.0)
    return dict(genome=genome, stem_weight=stem_weight, dilated_filter_weight=dilated_filter_weight, head_weight=head_weight, window_start=window_start, window_track=window_track, targets=targets)


def dilations(shard_rows):
    return (shard_rows // 8, shard_rows // 2, shard_rows, 2 * shard_rows, 4 * shard_rows)

def moved(field, offset):
    length = field.shape[-1]
    blanks = jnp.zeros(field.shape[:-1] + (abs(offset),), field.dtype)
    if offset > 0:
        return jnp.concatenate([field[..., offset:], blanks], axis=-1)
    return jnp.concatenate([blanks, field[..., :length + offset]], axis=-1)

def order_taps(lower_rows, middle, upper_rows):
    forward_taps = jnp.stack([lower_rows[0], middle[0], upper_rows[0]])
    reverse_taps = jnp.stack([upper_rows[1], middle[1], lower_rows[1]])
    return jnp.stack([forward_taps, reverse_taps])

def reference(genome, stem_weight, dilated_filter_weight, head_weight, window_start, window_track, targets):
    spans = dilations(ROWS)
    letters = (genome[:, :, None] == jnp.arange(4, dtype=jnp.int32)).astype(jnp.bfloat16).reshape(BINS, 4 * POOL)
    strands = jnp.stack([letters, letters[:, ::-1]])
    residual_state = jnp.einsum('sri,ci->scr', strands.astype(jnp.float32), stem_weight.astype(jnp.float32))
    saved_states = []
    stored_taps = []
    for current_layer_index in range(LAYERS):
        active = jax.nn.gelu(residual_state).astype(jnp.bfloat16)
        reach_now = spans[current_layer_index]
        resident_taps = order_taps(moved(active, -reach_now), active, moved(active, reach_now))
        saved_states.append(residual_state)
        stored_taps.append(resident_taps)
        residual_state = residual_state + jnp.einsum('nezp,efz->nfp', resident_taps.astype(jnp.float32), dilated_filter_weight[current_layer_index].astype(jnp.float32))
    strand_total = residual_state[0] + residual_state[1]
    positions = jnp.arange(BINS, dtype=jnp.int32)
    member = ((positions[None, :] >= window_start[:, None]) & (positions[None, :] < window_start[:, None] + WIN)).astype(jnp.float32)
    pooled = jnp.einsum('cr,kr->ck', strand_total, member, precision=lax.Precision.HIGHEST) / WIN
    columns = jnp.take(head_weight, window_track, axis=1).astype(jnp.float32)
    window_score = 0.5 * lax.optimization_barrier(jnp.sum(pooled * columns, axis=0))
    counts = lax.optimization_barrier(jnp.sum((window_track[:, None] == window_track[None, :]).astype(jnp.float32), axis=1))
    loss_slope = (jnp.exp(window_score) - targets) / counts
    head_grad = jnp.zeros(head_weight.shape, jnp.float32).at[:, window_track].add(0.5 * loss_slope[None, :] * pooled)
    weights_back = 0.5 / WIN * loss_slope[None, :] * columns
    back_total = jnp.einsum('ck,kr->cr', weights_back, member, precision=lax.Precision.HIGHEST)
    grad_state = jnp.stack([back_total, back_total])
    layer_gradient_list = []
    for current_layer_index in reversed(range(LAYERS)):
        incoming_gradient = grad_state.astype(jnp.bfloat16)
        layer_gradient_list.append(jnp.einsum('pygj,pij->yig', stored_taps[current_layer_index].astype(jnp.float32), incoming_gradient.astype(jnp.float32)))
        reach_now = spans[current_layer_index]
        back_taps = order_taps(moved(incoming_gradient, reach_now), incoming_gradient, moved(incoming_gradient, -reach_now))
        spread = jnp.einsum('skor,koc->scr', back_taps.astype(jnp.float32), dilated_filter_weight[current_layer_index].astype(jnp.float32))
        pullback = jax.vjp(jax.nn.gelu, saved_states[current_layer_index])[1]
        grad_state = grad_state + pullback(spread)[0]
    conv_grad = jnp.stack(layer_gradient_list[::-1])
    stem_grad = jnp.einsum('sri,scr->ci', strands.astype(jnp.float32), grad_state.astype(jnp.bfloat16).astype(jnp.float32))
    return (window_score, conv_grad, stem_grad, head_grad)
```

```python
import functools

import jax
import jax.numpy as jnp
from jax import lax
from jax.experimental import pallas as pl
from jax.experimental.pallas import tpu as pltpu
from jax.sharding import PartitionSpec as P

LAYERS = 5
WIN = 16
STEPS = (1, 4, 8, 16, 32)
MESH = pl.DeviceIdType.MESH
F32 = jnp.float32
BF16 = jnp.bfloat16
HIGH = lax.Precision.HIGHEST
NX, NY, NZ, NS, NC = 4, 4, 8, 32, 8
T = 256
C = 768
CX = 192
CD = 96
NW = 512
NL = 512
KO = 3 * CD
CZ = 24
ROOT = 0.7978845608028654
CUBE = 0.044715


def nt(a, b, **kw):
    return lax.dot_general(a, b, (((1,), (1,)), ((), ())), preferred_element_type=F32, **kw)


def tn(a, b):
    return lax.dot_general(a, b, (((0,), (0,)), ((), ())), preferred_element_type=F32)


def from_low(v, d):
    lane = lax.broadcasted_iota(jnp.int32, v.shape, 1)
    return jnp.where(lane >= d, pltpu.roll(v, d, 1), 0.0)


def from_high(v, d):
    lane = lax.broadcasted_iota(jnp.int32, v.shape, 1)
    return jnp.where(lane < v.shape[1] - d, pltpu.roll(v, v.shape[1] - d, 1), 0.0)


def tower(
    genome, stem, weight, cols_own, start, counts, targets,
    score_out, conv_out, stem_out, head_out,
    gen, gsend, grecv,
    stemw, colw, wst, local_sem, psend, precv,
    letters, act, act2, der, asend, arecv, a2send, a2recv,
    sone, ssone, rsone, stwo, sstwo, rstwo,
    part, bsend, brecv, bcomb, bs, br,
    up, upx, us, ur,
    wg, yrecv, ys, yr, zacc, zsend, zrecv, zs, zr,
    rin, rpart, rys, ryr, rzb, rgb, r_ps, r_pr, r_ys, r_yr, r_zs, r_zr, r_gs, r_gr,
):
    s = lax.axis_index("seq")
    c = lax.axis_index("ch")
    y = s // NZ
    z = s % NZ
    x = c // 2
    q = c % 2
    pc = 2 * x + (1 - q)
    pending = []

    def remote(src, dst, ssem, rsem, seq, ch):
        return pltpu.make_async_remote_copy(
            src_ref=src, dst_ref=dst, send_sem=ssem, recv_sem=rsem,
            device_id=(seq, ch), device_id_type=MESH,
        )

    def go(copy):
        copy.start()
        pending.append(copy)
        return copy

    def x_at(j):
        return 2 * ((x + j) % NX) + q

    def y_at(j):
        return ((y + j) % NY) * NZ + z

    def z_at(j):
        return y * NZ + (z + j) % NZ

    mine = pl.ds(pl.multiple_of(CD * q, CD), CD)
    other = pl.ds(pl.multiple_of(CD * (1 - q), CD), CD)

    local = [
        pltpu.make_async_copy(stem, stemw.at[mine], local_sem.at[0]),
        pltpu.make_async_copy(cols_own, colw.at[mine], local_sem.at[1]),
    ]
    for l in range(LAYERS):
        for k in range(3):
            local.append(
                pltpu.make_async_copy(
                    weight.at[l, k], wst.at[l, k + q * (2 - 2 * k), mine],
                    local_sem.at[2 + 3 * l + k],
                )
            )
    for copy in local:
        copy.start()

    barrier = pltpu.get_barrier_semaphore()

    def greet_seq(j, _):
        pl.semaphore_signal(barrier, inc=1, device_id=((s + j) % NS, c), device_id_type=MESH)
        return 0

    def greet_ch(j, _):
        pl.semaphore_signal(barrier, inc=1, device_id=(s, (c + j) % NC), device_id_type=MESH)
        return 0

    lax.fori_loop(1, NS, greet_seq, 0)
    lax.fori_loop(1, NC, greet_ch, 0)
    pl.semaphore_wait(barrier, NS - 1 + NC - 1)

    def gcopy(j):
        to = (s + j) % NS
        return remote(genome.at[to], gen.at[s], gsend.at[j], grecv.at[j], to, c)

    def gstart(j, _):
        gcopy(j).start()
        return 0

    def gwait(j, _):
        gcopy(j).wait_recv()
        return 0

    def gdone(j, _):
        gcopy(j).wait_send()
        return 0

    lax.fori_loop(1, NS, gstart, 0)
    pstem = go(remote(stem, stemw.at[mine], psend.at[0], precv.at[0], s, pc))
    pw = []
    for l in range(LAYERS):
        pw.append([
            go(remote(
                weight.at[l, k], wst.at[l, k + (1 - q) * (2 - 2 * k), mine],
                psend.at[2 + 3 * l + k], precv.at[2 + 3 * l + k], s, pc,
            ))
            for k in range(3)
        ])
    pcol = go(remote(cols_own, colw.at[mine], psend.at[1], precv.at[1], s, pc))

    gen[s] = genome[s]
    row = lax.broadcasted_iota(jnp.int32, (NL, NL), 0)
    col = lax.broadcasted_iota(jnp.int32, (NL, NL), 1)
    target = 4 * (col % 128) + col // 128
    target = jnp.where(q == 0, target, NL - 1 - target)
    order = (row == target).astype(F32).astype(BF16)
    lax.fori_loop(1, NS, gwait, 0)
    bases = gen[...].reshape(T, 128)
    hot = jnp.concatenate([(bases == n).astype(F32).astype(BF16) for n in range(4)], axis=1)
    letters[...] = nt(hot, order).astype(BF16)

    local[0].wait()
    pstem.wait_recv()
    state = nt(stemw[...], letters[...])

    a2 = []
    for l in range(LAYERS):
        d = STEPS[l]
        sq = state * state
        th = jnp.tanh(ROOT * state * (1.0 + CUBE * sq))
        half = 0.5 * (1.0 + th)
        a = (state * half).astype(BF16)
        act[l, x, 0] = a[:CD]
        act[l, x, 1] = a[CD:]

        def ring(slot, h, j, n):
            return go(remote(
                act.at[l, slot, h], act.at[l, slot, h], asend.at[l, n], arecv.at[l, n], s, x_at(j)
            ))

        f0 = ring(x, 0, 1, 0)
        b1 = ring(x, 1, 3, 1)
        f1 = ring(x, 1, 1, 2)
        b0 = ring(x, 0, 3, 3)
        der[l] = half + (0.5 * ROOT) * state * (1.0 - th * th) * (1.0 + (3 * CUBE) * sq)
        f0.wait_recv()
        fr = ring((x + 3) % NX, 0, 1, 4)
        b1.wait_recv()
        br_ = ring((x + 1) % NX, 1, 3, 5)
        for k in range(3):
            local[2 + 3 * l + k].wait()
            pw[l][k].wait_recv()
        f1.wait_recv()
        b0.wait_recv()
        fr.wait_recv()
        br_.wait_recv()
        a2.append(go(remote(act.at[l], act2.at[l], a2send.at[l], a2recv.at[l], s, pc)))
        p = jnp.dot(
            wst[l].reshape(3 * CX, C), act[l].reshape(C, T), preferred_element_type=F32
        )
        state = (
            state + p[CX:2 * CX] + from_low(p[:CX], d) + from_high(p[2 * CX:], d)
        )

    bins = NS * lax.broadcasted_iota(jnp.int32, (T, NW), 0) + s
    begin = start[...]
    member = ((bins >= begin) & (bins < begin + WIN)).astype(F32)
    pooled = jnp.dot(state, member, precision=HIGH, preferred_element_type=F32) / WIN
    local[1].wait()
    pcol.wait_recv()
    columns = colw[...].astype(F32)
    sone[c] = 0.5 * jnp.sum(pooled * columns, axis=0, keepdims=True)

    def one(j):
        to = (c + j) % NC
        return remote(sone.at[c], sone.at[c], ssone.at[j], rsone.at[j], s, to)

    ones = [go(one(j)) for j in range(1, NC)]

    def reduce_start(r, value):
        rin[r] = value
        return go(remote(rin.at[r, other], rpart.at[r], r_ps.at[r], r_pr.at[r], s, pc))

    def reduce_y(r, first):
        first.wait_recv()
        h = rin[r, mine] + rpart[r]
        for j in range(NY):
            rys[r, j] = h[:, 128 * j:128 * (j + 1)]
        return [
            go(remote(rys.at[r, (y + j) % NY], ryr.at[r, j], r_ys.at[r, j], r_yr.at[r, j], y_at(j), c))
            for j in range(1, NY)
        ]

    def reduce_z(r, copies):
        for copy in copies:
            copy.wait_recv()
        total = rys[r, y] + ryr[r, 1] + ryr[r, 2] + ryr[r, 3]
        rzb[r, z] = total.astype(BF16)
        return [
            go(remote(rzb.at[r, z], rzb.at[r, z], r_zs.at[r, j], r_zr.at[r, j], z_at(j), c))
            for j in range(1, NZ)
        ]

    def reduce_g(r, copies):
        for copy in copies:
            copy.wait_recv()
        total = rzb[r, 0].astype(F32)
        for j in range(1, NZ):
            total = total + rzb[r, j].astype(F32)
        rgb[r, y] = total
        return [
            go(remote(rgb.at[r, y], rgb.at[r, y], r_gs.at[r, j], r_gr.at[r, j], y_at(j), c))
            for j in range(1, NY)
        ]

    def reduce_end(r, copies):
        for copy in copies:
            copy.wait_recv()
        return jnp.concatenate([rgb[r, j] for j in range(NY)], axis=1)

    for copy in ones:
        copy.wait_recv()
    total = sone[0]
    for j in range(1, NC):
        total = total + sone[j]
    stwo[s] = total

    def two(j):
        to = (s + j) % NS
        return remote(stwo.at[s], stwo.at[s], sstwo.at[j], rstwo.at[j], to, c)

    def two_start(j, _):
        two(j).start()
        return 0

    def two_wait(j, _):
        two(j).wait_recv()
        return 0

    def two_done(j, _):
        two(j).wait_send()
        return 0

    lax.fori_loop(1, NS, two_start, 0)
    pool_copy = reduce_start(0, pooled)
    pool_copies = reduce_y(0, pool_copy)
    lax.fori_loop(1, NS, two_wait, 0)
    score = stwo[0]
    for j in range(1, NS):
        score = score + stwo[j]
    score_out[...] = score
    slope = (jnp.exp(score) - targets[...]) / counts[...]
    grad = nt((0.5 / WIN) * slope * columns, member, precision=HIGH)

    waiting_y = None
    waiting_z = []

    def y_stage(item):
        l, copies = item
        for copy in copies:
            copy.wait_recv()
        own = pl.ds(pl.multiple_of(CX * y, CX), CX)
        total = wg[l, own].astype(F32)
        for j in range(1, NY):
            total = total + yrecv[l, j].astype(F32)
        total = total.reshape(NZ, CZ, KO)
        zacc[l] = total
        zsend[l] = total.astype(BF16)
        sends = [
            go(remote(
                zsend.at[l, (z + j) % NZ], zrecv.at[l, j], zs.at[l, j], zr.at[l, j], z_at(j), c
            ))
            for j in range(1, NZ)
        ]
        waiting_z.append((l, sends))

    def z_stage(item):
        l, copies = item
        for copy in copies:
            copy.wait_recv()
        total = zacc[l, z]
        for j in range(1, NZ):
            total = total + zrecv[l, j].astype(F32)
        conv_out[l] = total

    for l in reversed(range(LAYERS)):
        d = STEPS[l]
        u = grad.astype(BF16)
        up[l] = u
        ucopy = go(remote(up.at[l, other], upx.at[l], us.at[l], ur.at[l], s, pc))
        u = u.astype(F32)
        taps = jnp.concatenate(
            [from_high(u, d).astype(BF16), u.astype(BF16), from_low(u, d).astype(BF16)], axis=0
        )
        p = tn(wst[l].reshape(3 * CX, C), taps)
        part[...] = p
        for i in range(NX):
            for h in range(2):
                at = CX * i + CD * h
                bsend[l, i, h] = p[at:at + CD].astype(BF16)

        def shed(src, n, j):
            return go(remote(src, brecv.at[l, n], bs.at[l, n], br.at[l, n], s, x_at(j)))

        far = (x + 2) % NX
        right = (x + 1) % NX
        left = (x + 3) % NX
        f1 = shed(bsend.at[l, far, 1], 0, 1)
        b0 = shed(bsend.at[l, far, 0], 1, 3)
        f0 = shed(bsend.at[l, right, 0], 2, 1)
        b1 = shed(bsend.at[l, left, 1], 3, 3)
        ucopy.wait_recv()
        a2[l].wait_recv()
        v = up[l, mine].astype(F32)
        w = upx[l].astype(F32)
        vh, vl = from_high(v, d).astype(BF16), from_low(v, d).astype(BF16)
        wh, wl = from_high(w, d).astype(BF16), from_low(w, d).astype(BF16)
        first = q == 0
        own_taps = jnp.concatenate(
            [jnp.where(first, vh, vl), v.astype(BF16), jnp.where(first, vl, vh)], axis=0
        )
        far_taps = jnp.concatenate(
            [jnp.where(first, wl, wh), w.astype(BF16), jnp.where(first, wh, wl)], axis=0
        )
        f1.wait_recv()
        b0.wait_recv()
        at = pl.ds(pl.multiple_of(CX * right + CD, CD), CD)
        bcomb[l, 0] = (part[at] + brecv[l, 0].astype(F32)).astype(BF16)
        fc = shed(bcomb.at[l, 0], 4, 1)
        at = pl.ds(pl.multiple_of(CX * left, CD), CD)
        bcomb[l, 1] = (part[at] + brecv[l, 1].astype(F32)).astype(BF16)
        bc = shed(bcomb.at[l, 1], 5, 3)

        g = nt(act[l].reshape(C, T), own_taps) + nt(act2[l].reshape(C, T), far_taps)
        wg[l] = g.astype(BF16)
        ysends = [
            go(remote(
                wg.at[l, pl.ds(pl.multiple_of(CX * ((y + j) % NY), CX), CX)], yrecv.at[l, j],
                ys.at[l, j], yr.at[l, j], y_at(j), c,
            ))
            for j in range(1, NY)
        ]
        if waiting_y is not None:
            y_stage(waiting_y)
        waiting_y = (l, ysends)
        if len(waiting_z) > 1:
            z_stage(waiting_z.pop(0))
        if l == LAYERS - 1:
            pool_copies = reduce_z(0, pool_copies)
        if l == LAYERS - 3:
            pool_copies = reduce_g(0, pool_copies)
        f0.wait_recv()
        b1.wait_recv()
        fc.wait_recv()
        bc.wait_recv()
        own0 = part[pl.ds(pl.multiple_of(CX * x, CD), CD)]
        own1 = part[pl.ds(pl.multiple_of(CX * x + CD, CD), CD)]
        low = own0 + brecv[l, 2].astype(F32) + brecv[l, 5].astype(F32)
        high = own1 + brecv[l, 3].astype(F32) + brecv[l, 4].astype(F32)
        grad = grad + jnp.concatenate([low, high], axis=0) * der[l]

    stem_copy = reduce_start(
        1, jnp.dot(grad.astype(BF16), letters[...], preferred_element_type=F32)
    )
    stem_copies = reduce_y(1, stem_copy)
    y_stage(waiting_y)
    z_stage(waiting_z.pop(0))
    total = reduce_end(0, pool_copies)
    head_out[...] = 0.5 * slope * total
    stem_copies = reduce_z(1, stem_copies)
    while waiting_z:
        z_stage(waiting_z.pop(0))
    stem_copies = reduce_g(1, stem_copies)
    stem_out[...] = reduce_end(1, stem_copies)

    lax.fori_loop(1, NS, gdone, 0)
    lax.fori_loop(1, NS, two_done, 0)
    for copy in pending:
        copy.wait_send()


def shards(
    genome, stem_weight, dilated_filter_weight, head_weight, window_start, window_track, targets
):
    bins = genome.reshape(T // NS, NS, 128).transpose(1, 0, 2)
    columns = jnp.take(head_weight, window_track, axis=1)
    counts = jnp.sum(
        (window_track[:, None] == window_track[None, :]).astype(F32), axis=0, keepdims=True
    )
    dma = pltpu.SemaphoreType.DMA
    V = pltpu.VMEM
    scratch = [
        V((NS, T // NS, 128), jnp.int32), dma((NS,)), dma((NS,)),
        V((CX, NL), BF16), V((CX, NW), BF16), V((LAYERS, 3, CX, C), BF16),
        dma((17,)), dma((17,)), dma((17,)),
        V((T, NL), BF16),
        V((LAYERS, NX, 2, CD, T), BF16), V((LAYERS, NX, 2, CD, T), BF16),
        V((LAYERS, CX, T), F32), dma((LAYERS, 6)), dma((LAYERS, 6)),
        dma((LAYERS,)), dma((LAYERS,)),
        V((NC, 1, NW), F32), dma((NC,)), dma((NC,)),
        V((NS, 1, NW), F32), dma((NS,)), dma((NS,)),
        V((C, T), F32), V((LAYERS, NX, 2, CD, T), BF16), V((LAYERS, 6, CD, T), BF16),
        V((LAYERS, 2, CD, T), BF16), dma((LAYERS, 6)), dma((LAYERS, 6)),
        V((LAYERS, CX, T), BF16), V((LAYERS, CD, T), BF16), dma((LAYERS,)), dma((LAYERS,)),
        V((LAYERS, C, KO), BF16), V((LAYERS, NY, CX, KO), BF16),
        dma((LAYERS, NY)), dma((LAYERS, NY)),
        V((LAYERS, NZ, CZ, KO), F32), V((LAYERS, NZ, CZ, KO), BF16),
        V((LAYERS, NZ, CZ, KO), BF16), dma((LAYERS, NZ)), dma((LAYERS, NZ)),
        V((2, CX, NW), F32), V((2, CD, NW), F32), V((2, NY, CD, 128), F32),
        V((2, NY, CD, 128), F32), V((2, NZ, CD, 128), BF16), V((2, NY, CD, 128), F32),
        dma((2,)), dma((2,)), dma((2, NY)), dma((2, NY)), dma((2, NZ)), dma((2, NZ)),
        dma((2, NY)), dma((2, NY)),
    ]
    vm = pl.BlockSpec(memory_space=pltpu.VMEM)
    hbm = pl.BlockSpec(memory_space=pl.ANY)
    score, conv, stem_grad, terms = pl.pallas_call(
        tower,
        out_shape=(
            jax.ShapeDtypeStruct((1, NW), F32),
            jax.ShapeDtypeStruct((LAYERS, CZ, KO), F32),
            jax.ShapeDtypeStruct((CD, NL), F32),
            jax.ShapeDtypeStruct((CD, NW), F32),
        ),
        in_specs=[vm, hbm, hbm, hbm, vm, vm, vm],
        out_specs=(vm, vm, vm, vm),
        scratch_shapes=scratch,
        compiler_params=pltpu.CompilerParams(
            collective_id=0, has_side_effects=True, vmem_limit_bytes=60 * 1024 * 1024
        ),
    )(
        bins, stem_weight, dilated_filter_weight, columns,
        window_start.reshape(1, NW), counts, targets.reshape(1, NW),
    )
    conv_grad = conv.reshape(LAYERS, CZ, 3, CD).transpose(0, 2, 3, 1)
    head_grad = jnp.zeros(head_weight.shape, F32).at[:, window_track].add(terms)
    return (score.reshape(NW), conv_grad, stem_grad, head_grad)


def solution(mesh):
    return jax.shard_map(
        shards,
        mesh=mesh,
        in_specs=(
            P("seq", None),
            P("ch", None),
            P(None, None, "ch", None),
            P("ch", None),
            P(),
            P(),
            P(),
        ),
        out_specs=(P(), P(None, None, "ch", "seq"), P("ch", None), P("ch", None)),
        check_vma=False,
    )
```

```python
import functools

import jax
import jax.numpy as jnp
from jax import lax
from jax.experimental import pallas as pl
from jax.experimental.pallas import tpu as pltpu
from jax.sharding import PartitionSpec as P

LAYERS = 5
WIN = 16
STEPS = (1, 4, 8, 16, 32)
MESH = pl.DeviceIdType.MESH
F32 = jnp.float32
BF16 = jnp.bfloat16
HIGH = lax.Precision.HIGHEST
NX, NY, NZ, NS, NC = 4, 4, 8, 32, 8
T = 256
C = 768
CX = 192
CD = 96
NW = 512
NL = 512
KO = 3 * CD
CZ = 24
TRACKS = 5313
CHUNK = 512
WHOLE = TRACKS // CHUNK
REST = TRACKS - WHOLE * CHUNK
ROOT = 0.7978845608028654
CUBE = 0.044715


def nt(a, b, **kw):
    return lax.dot_general(a, b, (((1,), (1,)), ((), ())), preferred_element_type=F32, **kw)


def tn(a, b):
    return lax.dot_general(a, b, (((0,), (0,)), ((), ())), preferred_element_type=F32)


def from_low(v, d):
    lane = lax.broadcasted_iota(jnp.int32, v.shape, 1)
    return jnp.where(lane >= d, pltpu.roll(v, d, 1), 0.0)


def from_high(v, d):
    lane = lax.broadcasted_iota(jnp.int32, v.shape, 1)
    return jnp.where(lane < v.shape[1] - d, pltpu.roll(v, v.shape[1] - d, 1), 0.0)


def tower(
    genome, stem, weight, head, start, track, targets,
    score_out, conv_out, stem_out, head_out,
    gbuf, gen, gsend, grecv, headw,
    stemw, colw, wst, local_sem, psend, precv,
    letters, act, act2, der, asend, arecv, a2send, a2recv,
    sone, ssone, rsone, stwo, sstwo, rstwo,
    part, bsend, brecv, bcomb, bs, br,
    up, upx, us, ur,
    wg, yrecv, ys, yr, zacc, zsend, zrecv, zs, zr,
    rys, ryr, rzb, rgb, r_ys, r_yr, r_zs, r_zr, r_gs, r_gr, thirds,
):
    s = lax.axis_index("seq")
    c = lax.axis_index("ch")
    y = s // NZ
    z = s % NZ
    x = c // 2
    q = c % 2
    pc = 2 * x + (1 - q)
    pending = []

    def one_hot(base, width):
        ids = lax.broadcasted_iota(jnp.int32, (width, NW), 0) + base
        return (ids == track[...]).astype(F32).astype(BF16)

    def chunk(i):
        return pl.ds(pl.multiple_of(i * CHUNK, CHUNK), CHUNK)

    def remote(src, dst, ssem, rsem, seq, ch):
        return pltpu.make_async_remote_copy(
            src_ref=src, dst_ref=dst, send_sem=ssem, recv_sem=rsem,
            device_id=(seq, ch), device_id_type=MESH,
        )

    def go(copy):
        copy.start()
        pending.append(copy)
        return copy

    def lead(copy):
        pending[:] = [p for p in pending if p is not copy]
        copy.wait_send()

    def x_at(j):
        return 2 * ((x + j) % NX) + q

    def y_at(j):
        return ((y + j) % NY) * NZ + z

    def z_at(j):
        return y * NZ + (z + j) % NZ

    mine = pl.ds(pl.multiple_of(CD * q, CD), CD)
    other = pl.ds(pl.multiple_of(CD * (1 - q), CD), CD)

    local = [
        pltpu.make_async_copy(stem, stemw.at[mine], local_sem.at[0]),
        pltpu.make_async_copy(head, headw, local_sem.at[1]),
    ]
    for l in range(LAYERS):
        for k in range(3):
            local.append(
                pltpu.make_async_copy(
                    weight.at[l, k], wst.at[l, k + q * (2 - 2 * k), mine],
                    local_sem.at[2 + 3 * l + k],
                )
            )
    for copy in local:
        copy.start()

    barrier = pltpu.get_barrier_semaphore()

    def greet_seq(j, _):
        pl.semaphore_signal(barrier, inc=1, device_id=((s + j) % NS, c), device_id_type=MESH)
        return 0

    def greet_ch(j, _):
        pl.semaphore_signal(barrier, inc=1, device_id=(s, (c + j) % NC), device_id_type=MESH)
        return 0

    lax.fori_loop(1, NS, greet_seq, 0)
    lax.fori_loop(1, NC, greet_ch, 0)
    for j in range(1, NY):
        pl.semaphore_signal(barrier, inc=1, device_id=(y_at(j), pc), device_id_type=MESH)
    for r in range(NS):
        gbuf[r] = genome[pl.ds(r, T // NS, stride=NS), :]
    pl.semaphore_wait(barrier, NS - 1 + NC - 1 + NY - 1)

    def gcopy(j):
        to = (s + j) % NS
        return remote(gbuf.at[to], gen.at[s], gsend.at[j], grecv.at[j], to, c)

    def gstart(j, _):
        gcopy(j).start()
        return 0

    def gwait(j, _):
        gcopy(j).wait_recv()
        return 0

    def gdone(j, _):
        gcopy(j).wait_send()
        return 0

    lax.fori_loop(1, NS, gstart, 0)
    pstem = go(remote(stem, stemw.at[mine], psend.at[0], precv.at[0], s, pc))
    pw = []
    for l in range(LAYERS):
        pw.append([
            go(remote(
                weight.at[l, k], wst.at[l, k + (1 - q) * (2 - 2 * k), mine],
                psend.at[2 + 3 * l + k], precv.at[2 + 3 * l + k], s, pc,
            ))
            for k in range(3)
        ])

    gen[s] = gbuf[s]
    local[1].wait()

    def pick(i, total):
        return total + jnp.dot(
            headw[:, chunk(i)], one_hot(i * CHUNK, CHUNK), preferred_element_type=F32
        )

    picked = lax.fori_loop(0, WHOLE, pick, jnp.zeros((CD, NW), F32))
    picked = picked + jnp.dot(
        headw[:, WHOLE * CHUNK:], one_hot(WHOLE * CHUNK, REST), preferred_element_type=F32
    )
    colw[mine] = picked.astype(BF16)
    pcol = go(remote(colw.at[mine], colw.at[mine], psend.at[1], precv.at[1], s, pc))
    tracks = jnp.broadcast_to(track[...].astype(F32), (8, NW))
    across = jnp.transpose(tracks)[:, :1]
    counts = jnp.sum((across == tracks[:1]).astype(F32), axis=0, keepdims=True)
    row = lax.broadcasted_iota(jnp.int32, (NL, NL), 0)
    col = lax.broadcasted_iota(jnp.int32, (NL, NL), 1)
    target = 4 * (col % 128) + col // 128
    target = jnp.where(q == 0, target, NL - 1 - target)
    order = (row == target).astype(F32).astype(BF16)
    lax.fori_loop(1, NS, gwait, 0)
    bases = gen[...].reshape(T, 128)
    hot = jnp.concatenate([(bases == n).astype(F32).astype(BF16) for n in range(4)], axis=1)
    letters[...] = nt(hot, order).astype(BF16)

    local[0].wait()
    pstem.wait_recv()
    state = nt(stemw[...], letters[...])

    def share(l):
        return go(remote(act.at[l], act2.at[l], a2send.at[l], a2recv.at[l], s, pc))

    for l in range(LAYERS):
        d = STEPS[l]
        sq = state * state
        th = jnp.tanh(ROOT * state * (1.0 + CUBE * sq))
        half = 0.5 * (1.0 + th)
        a = (state * half).astype(BF16)
        act[l, x, 0] = a[:CD]
        act[l, x, 1] = a[CD:]

        def ring(slot, h, j, n):
            return go(remote(
                act.at[l, slot, h], act.at[l, slot, h], asend.at[l, n], arecv.at[l, n], s, x_at(j)
            ))

        f0 = ring(x, 0, 1, 0)
        b1 = ring(x, 1, 3, 1)
        der[l] = half + (0.5 * ROOT) * state * (1.0 - th * th) * (1.0 + (3 * CUBE) * sq)
        lead(f0)
        f1 = ring(x, 1, 1, 2)
        lead(b1)
        b0 = ring(x, 0, 3, 3)
        f0.wait_recv()
        fr = ring((x + 3) % NX, 0, 1, 4)
        b1.wait_recv()
        br_ = ring((x + 1) % NX, 1, 3, 5)
        for k in range(3):
            local[2 + 3 * l + k].wait()
            pw[l][k].wait_recv()
        f1.wait_recv()
        b0.wait_recv()
        fr.wait_recv()
        br_.wait_recv()
        p = jnp.dot(
            wst[l].reshape(3 * CX, C), act[l].reshape(C, T), preferred_element_type=F32
        )
        state = (
            state + p[CX:2 * CX] + from_low(p[:CX], d) + from_high(p[2 * CX:], d)
        )

    bins = NS * lax.broadcasted_iota(jnp.int32, (T, NW), 0) + s
    begin = start[...]
    member = ((bins >= begin) & (bins < begin + WIN)).astype(F32)
    pooled = jnp.dot(state, member, precision=HIGH, preferred_element_type=F32) / WIN
    pcol.wait_recv()
    columns = colw[...].astype(F32)
    sone[c] = 0.5 * jnp.sum(pooled * columns, axis=0, keepdims=True)

    def one(j):
        to = (c + j) % NC
        return remote(sone.at[c], sone.at[c], ssone.at[j], rsone.at[j], s, to)

    ones = [go(one(j)) for j in range(1, NC)]

    def reduce_y(r, value):
        for i in range(2):
            for j in range(NY):
                rys[r, i, j] = value[CD * i:CD * (i + 1), 128 * j:128 * (j + 1)].astype(BF16)
        return [
            go(remote(
                rys.at[r, (q + i) % 2, (y + j) % NY], ryr.at[r, NY * i + j],
                r_ys.at[r, NY * i + j], r_yr.at[r, NY * i + j], y_at(j), 2 * x + (q + i) % 2,
            ))
            for j in range(NY) for i in range(2) if i + j > 0
        ]

    def reduce_z(r, copies):
        for copy in copies:
            copy.wait_recv()
        total = rys[r, q, y].astype(F32)
        for i in range(1, 2 * NY):
            total = total + ryr[r, i].astype(F32)
        rzb[r, z] = total.astype(BF16)
        return [
            go(remote(rzb.at[r, z], rzb.at[r, z], r_zs.at[r, j], r_zr.at[r, j], z_at(j), c))
            for j in range(1, NZ)
        ]

    def reduce_g(r, copies):
        for copy in copies:
            copy.wait_recv()
        total = rzb[r, 0].astype(F32)
        for j in range(1, NZ):
            total = total + rzb[r, j].astype(F32)
        rgb[r, y] = total
        return [
            go(remote(rgb.at[r, y], rgb.at[r, y], r_gs.at[r, j], r_gr.at[r, j], y_at(j), c))
            for j in range(1, NY)
        ]

    def reduce_end(r, copies):
        for copy in copies:
            copy.wait_recv()
        return jnp.concatenate([rgb[r, j] for j in range(NY)], axis=1)

    for copy in ones:
        copy.wait_recv()
    total = sone[0]
    for j in range(1, NC):
        total = total + sone[j]
    stwo[s] = total

    def two(j):
        to = (s + j) % NS
        return remote(stwo.at[s], stwo.at[s], sstwo.at[j], rstwo.at[j], to, c)

    def two_start(j, _):
        two(j).start()
        return 0

    def two_wait(j, _):
        two(j).wait_recv()
        return 0

    def two_done(j, _):
        two(j).wait_send()
        return 0

    lax.fori_loop(1, NS, two_start, 0)
    pool_copies = reduce_y(0, pooled)
    a2 = {4: share(4), 3: share(3)}
    lax.fori_loop(1, NS, two_wait, 0)
    score = stwo[0]
    for j in range(1, NS):
        score = score + stwo[j]
    score_out[...] = score
    slope = (jnp.exp(score) - targets[...]) / counts
    grad = nt((0.5 / WIN) * slope * columns, member, precision=HIGH)

    waiting_y = None
    waiting_z = []

    def y_stage(item):
        l, copies = item
        for copy in copies:
            copy.wait_recv()
        own = pl.ds(pl.multiple_of(CX * y, CX), CX)
        total = wg[l, own].astype(F32)
        for j in range(1, NY):
            total = total + yrecv[l, j].astype(F32)
        total = total.reshape(NZ, CZ, KO)
        zacc[l] = total
        zsend[l] = total.astype(BF16)
        sends = [
            go(remote(
                zsend.at[l, (z + j) % NZ], zrecv.at[l, j], zs.at[l, j], zr.at[l, j], z_at(j), c
            ))
            for j in range(1, NZ)
        ]
        waiting_z.append((l, sends))

    def z_stage(item):
        l, copies = item
        for copy in copies:
            copy.wait_recv()
        total = zacc[l, z]
        for j in range(1, NZ):
            total = total + zrecv[l, j].astype(F32)
        conv_out[l] = jnp.transpose(total).reshape(3, CD, CZ)

    def place(first, last):
        def body(i, _):
            head_out[:, chunk(i)] = spread_out(one_hot(i * CHUNK, CHUNK))
            return 0

        lax.fori_loop(first, last, body, 0)

    def spread_out(hot):
        out = nt(thirds[...], hot)
        return out[:CD] + out[CD:2 * CD] + out[2 * CD:]

    for l in reversed(range(LAYERS)):
        d = STEPS[l]
        u = grad.astype(BF16)
        up[l] = u
        ucopy = go(remote(up.at[l, other], upx.at[l], us.at[l], ur.at[l], s, pc))
        u = u.astype(F32)
        taps = jnp.concatenate(
            [from_high(u, d).astype(BF16), u.astype(BF16), from_low(u, d).astype(BF16)], axis=0
        )
        p = tn(wst[l].reshape(3 * CX, C), taps)
        part[...] = p
        for i in range(NX):
            for h in range(2):
                at = CX * i + CD * h
                bsend[l, i, h] = p[at:at + CD].astype(BF16)

        def shed(src, n, j):
            return go(remote(src, brecv.at[l, n], bs.at[l, n], br.at[l, n], s, x_at(j)))

        far = (x + 2) % NX
        right = (x + 1) % NX
        left = (x + 3) % NX
        f1 = shed(bsend.at[l, far, 1], 0, 1)
        b0 = shed(bsend.at[l, far, 0], 1, 3)
        if l >= 2:
            a2[l - 2] = share(l - 2)
        first = q == 0
        v = up[l, mine].astype(F32)
        vh, vl = from_high(v, d).astype(BF16), from_low(v, d).astype(BF16)
        own_taps = jnp.concatenate(
            [jnp.where(first, vh, vl), v.astype(BF16), jnp.where(first, vl, vh)], axis=0
        )
        g = nt(act[l].reshape(C, T), own_taps)
        lead(f1)
        f0 = shed(bsend.at[l, right, 0], 2, 1)
        lead(b0)
        b1 = shed(bsend.at[l, left, 1], 3, 3)
        ucopy.wait_recv()
        a2[l].wait_recv()
        w = upx[l].astype(F32)
        wh, wl = from_high(w, d).astype(BF16), from_low(w, d).astype(BF16)
        far_taps = jnp.concatenate(
            [jnp.where(first, wl, wh), w.astype(BF16), jnp.where(first, wh, wl)], axis=0
        )
        wg[l] = (g + nt(act2[l].reshape(C, T), far_taps)).astype(BF16)
        ysends = [
            go(remote(
                wg.at[l, pl.ds(pl.multiple_of(CX * ((y + j) % NY), CX), CX)], yrecv.at[l, j],
                ys.at[l, j], yr.at[l, j], y_at(j), c,
            ))
            for j in range(1, NY)
        ]
        f1.wait_recv()
        b0.wait_recv()
        at = pl.ds(pl.multiple_of(CX * right + CD, CD), CD)
        bcomb[l, 0] = (part[at] + brecv[l, 0].astype(F32)).astype(BF16)
        fc = shed(bcomb.at[l, 0], 4, 1)
        at = pl.ds(pl.multiple_of(CX * left, CD), CD)
        bcomb[l, 1] = (part[at] + brecv[l, 1].astype(F32)).astype(BF16)
        bc = shed(bcomb.at[l, 1], 5, 3)
        if waiting_y is not None:
            y_stage(waiting_y)
        waiting_y = (l, ysends)
        if len(waiting_z) > 1:
            z_stage(waiting_z.pop(0))
        if l == LAYERS - 1:
            pool_copies = reduce_z(0, pool_copies)
        if l == LAYERS - 2:
            pool_copies = reduce_g(0, pool_copies)
        if l == LAYERS - 3:
            terms = 0.5 * slope * reduce_end(0, pool_copies)
            for i in range(3):
                piece = terms.astype(BF16)
                thirds[CD * i:CD * (i + 1)] = piece
                terms = terms - piece.astype(F32)
            place(0, WHOLE // 2)
        if l == LAYERS - 4:
            place(WHOLE // 2, WHOLE)
            head_out[:, WHOLE * CHUNK:] = spread_out(one_hot(WHOLE * CHUNK, REST))
        f0.wait_recv()
        b1.wait_recv()
        fc.wait_recv()
        bc.wait_recv()
        own0 = part[pl.ds(pl.multiple_of(CX * x, CD), CD)]
        own1 = part[pl.ds(pl.multiple_of(CX * x + CD, CD), CD)]
        low = own0 + brecv[l, 2].astype(F32) + brecv[l, 5].astype(F32)
        high = own1 + brecv[l, 3].astype(F32) + brecv[l, 4].astype(F32)
        grad = grad + jnp.concatenate([low, high], axis=0) * der[l]

    stem_copies = reduce_y(
        1, jnp.dot(grad.astype(BF16), letters[...], preferred_element_type=F32)
    )
    y_stage(waiting_y)
    z_stage(waiting_z.pop(0))
    stem_copies = reduce_z(1, stem_copies)
    while waiting_z:
        z_stage(waiting_z.pop(0))
    stem_copies = reduce_g(1, stem_copies)
    stem_out[...] = reduce_end(1, stem_copies)

    lax.fori_loop(1, NS, gdone, 0)
    lax.fori_loop(1, NS, two_done, 0)
    for copy in pending:
        copy.wait_send()


def shards(
    genome, stem_weight, dilated_filter_weight, head_weight, window_start, window_track, targets
):
    dma = pltpu.SemaphoreType.DMA
    V = pltpu.VMEM
    scratch = [
        V((NS, T // NS, 128), jnp.int32), V((NS, T // NS, 128), jnp.int32), dma((NS,)), dma((NS,)),
        V((CD, TRACKS), BF16),
        V((CX, NL), BF16), V((CX, NW), BF16), V((LAYERS, 3, CX, C), BF16),
        dma((17,)), dma((17,)), dma((17,)),
        V((T, NL), BF16),
        V((LAYERS, NX, 2, CD, T), BF16), V((LAYERS, NX, 2, CD, T), BF16),
        V((LAYERS, CX, T), F32), dma((LAYERS, 6)), dma((LAYERS, 6)),
        dma((LAYERS,)), dma((LAYERS,)),
        V((NC, 1, NW), F32), dma((NC,)), dma((NC,)),
        V((NS, 1, NW), F32), dma((NS,)), dma((NS,)),
        V((C, T), F32), V((LAYERS, NX, 2, CD, T), BF16), V((LAYERS, 6, CD, T), BF16),
        V((LAYERS, 2, CD, T), BF16), dma((LAYERS, 6)), dma((LAYERS, 6)),
        V((LAYERS, CX, T), BF16), V((LAYERS, CD, T), BF16), dma((LAYERS,)), dma((LAYERS,)),
        V((LAYERS, C, KO), BF16), V((LAYERS, NY, CX, KO), BF16),
        dma((LAYERS, NY)), dma((LAYERS, NY)),
        V((LAYERS, NZ, CZ, KO), F32), V((LAYERS, NZ, CZ, KO), BF16),
        V((LAYERS, NZ, CZ, KO), BF16), dma((LAYERS, NZ)), dma((LAYERS, NZ)),
        V((2, 2, NY, CD, 128), BF16), V((2, 2 * NY, CD, 128), BF16),
        V((2, NZ, CD, 128), BF16), V((2, NY, CD, 128), F32),
        dma((2, 2 * NY)), dma((2, 2 * NY)), dma((2, NZ)), dma((2, NZ)),
        dma((2, NY)), dma((2, NY)), V((KO, NW), BF16),
    ]
    vm = pl.BlockSpec(memory_space=pltpu.VMEM)
    hbm = pl.BlockSpec(memory_space=pl.ANY)
    score, conv_grad, stem_grad, head_grad = pl.pallas_call(
        tower,
        out_shape=(
            jax.ShapeDtypeStruct((1, NW), F32),
            jax.ShapeDtypeStruct((LAYERS, 3, CD, CZ), F32),
            jax.ShapeDtypeStruct((CD, NL), F32),
            jax.ShapeDtypeStruct((CD, TRACKS), F32),
        ),
        in_specs=[vm, hbm, hbm, hbm, vm, vm, vm],
        out_specs=(vm, vm, vm, vm),
        scratch_shapes=scratch,
        compiler_params=pltpu.CompilerParams(
            collective_id=0, has_side_effects=True, vmem_limit_bytes=60 * 1024 * 1024
        ),
    )(
        genome, stem_weight, dilated_filter_weight, head_weight,
        window_start.reshape(1, NW), window_track.reshape(1, NW), targets.reshape(1, NW),
    )
    return (score.reshape(NW), conv_grad, stem_grad, head_grad)


def solution(mesh):
    return jax.shard_map(
        shards,
        mesh=mesh,
        in_specs=(
            P("seq", None),
            P("ch", None),
            P(None, None, "ch", None),
            P("ch", None),
            P(),
            P(),
            P(),
        ),
        out_specs=(P(), P(None, None, "ch", "seq"), P("ch", None), P("ch", None)),
        check_vma=False,
    )
```

```python
import functools

import jax
import jax.numpy as jnp
from jax import lax
from jax.experimental import pallas as pl
from jax.experimental.pallas import tpu as pltpu
from jax.sharding import PartitionSpec as P

LAYERS = 5
WIN = 16
STEPS = (1, 4, 8, 16, 32)
MESH = pl.DeviceIdType.MESH
F32 = jnp.float32
BF16 = jnp.bfloat16
HIGH = lax.Precision.HIGHEST
NX, NY, NZ, NS, NC = 4, 4, 8, 32, 8
T = 256
C = 768
CX = 192
CD = 96
NW = 512
NL = 512
KO = 3 * CD
CZ = 24
TRACKS = 5313
CHUNK = 512
WHOLE = TRACKS // CHUNK
REST = TRACKS - WHOLE * CHUNK
ROOT = 0.7978845608028654
CUBE = 0.044715


def nt(a, b, **kw):
    return lax.dot_general(a, b, (((1,), (1,)), ((), ())), preferred_element_type=F32, **kw)


def tn(a, b):
    return lax.dot_general(a, b, (((0,), (0,)), ((), ())), preferred_element_type=F32)


def from_low(v, d):
    lane = lax.broadcasted_iota(jnp.int32, v.shape, 1)
    return jnp.where(lane >= d, pltpu.roll(v, d, 1), 0.0)


def from_high(v, d):
    lane = lax.broadcasted_iota(jnp.int32, v.shape, 1)
    return jnp.where(lane < v.shape[1] - d, pltpu.roll(v, v.shape[1] - d, 1), 0.0)


def tower(
    genome, stem, weight, head, start, track, targets,
    score_out, conv_out, stem_out, head_out,
    gbuf, gen, gsend, grecv, headw,
    stemw, colw, wst, local_sem, psend, precv,
    letters, act, act2, der, asend, arecv, a2send, a2recv,
    sone, ssone, rsone, stwo, sstwo, rstwo,
    part, bsend, brecv, bcomb, bs, br,
    up, upx, us, ur,
    wg, yrecv, ys, yr, zacc, zsend, zrecv, zs, zr,
    rys, ryr, rzb, rgb, r_ys, r_yr, r_zs, r_zr, r_gs, r_gr, thirds,
):
    s = lax.axis_index("seq")
    c = lax.axis_index("ch")
    y = s // NZ
    z = s % NZ
    x = c // 2
    q = c % 2
    pc = 2 * x + (1 - q)
    pending = []

    def one_hot(base, width):
        ids = lax.broadcasted_iota(jnp.int32, (width, NW), 0) + base
        return (ids == track[...]).astype(F32).astype(BF16)

    def chunk(i):
        return pl.ds(pl.multiple_of(i * CHUNK, CHUNK), CHUNK)

    def remote(src, dst, ssem, rsem, seq, ch):
        return pltpu.make_async_remote_copy(
            src_ref=src, dst_ref=dst, send_sem=ssem, recv_sem=rsem,
            device_id=(seq, ch), device_id_type=MESH,
        )

    def go(copy):
        copy.start()
        pending.append(copy)
        return copy

    def lead(copy):
        pending[:] = [p for p in pending if p is not copy]
        copy.wait_send()

    def x_at(j):
        return 2 * ((x + j) % NX) + q

    def y_at(j):
        return ((y + j) % NY) * NZ + z

    def z_at(j):
        return y * NZ + (z + j) % NZ

    mine = pl.ds(pl.multiple_of(CD * q, CD), CD)
    other = pl.ds(pl.multiple_of(CD * (1 - q), CD), CD)

    local = [
        pltpu.make_async_copy(stem, stemw.at[mine], local_sem.at[0]),
        pltpu.make_async_copy(head, headw, local_sem.at[1]),
    ]
    for l in range(LAYERS):
        for k in range(3):
            local.append(
                pltpu.make_async_copy(
                    weight.at[l, k], wst.at[l, k + q * (2 - 2 * k), mine],
                    local_sem.at[2 + 3 * l + k],
                )
            )
    for copy in local:
        copy.start()

    barrier = pltpu.get_barrier_semaphore()

    def greet_seq(j, _):
        pl.semaphore_signal(barrier, inc=1, device_id=((s + j) % NS, c), device_id_type=MESH)
        return 0

    def greet_ch(j, _):
        pl.semaphore_signal(barrier, inc=1, device_id=(s, (c + j) % NC), device_id_type=MESH)
        return 0

    lax.fori_loop(1, NS, greet_seq, 0)
    lax.fori_loop(1, NC, greet_ch, 0)
    for j in range(1, NY):
        pl.semaphore_signal(barrier, inc=1, device_id=(y_at(j), pc), device_id_type=MESH)
    for r in range(NS):
        gbuf[r] = genome[pl.ds(r, T // NS, stride=NS), :]
    pl.semaphore_wait(barrier, NS - 1 + NC - 1 + NY - 1)

    def gcopy(j):
        to = (s + j) % NS
        return remote(gbuf.at[to], gen.at[s], gsend.at[j], grecv.at[j], to, c)

    def gstart(j, _):
        gcopy(j).start()
        return 0

    def gwait(j, _):
        gcopy(j).wait_recv()
        return 0

    def gdone(j, _):
        gcopy(j).wait_send()
        return 0

    lax.fori_loop(1, NS, gstart, 0)
    pstem = go(remote(stem, stemw.at[mine], psend.at[0], precv.at[0], s, pc))
    pw = []
    for l in range(LAYERS):
        pw.append([
            go(remote(
                weight.at[l, k], wst.at[l, k + (1 - q) * (2 - 2 * k), mine],
                psend.at[2 + 3 * l + k], precv.at[2 + 3 * l + k], s, pc,
            ))
            for k in range(3)
        ])

    gen[s] = gbuf[s]
    local[1].wait()

    def pick(i, total):
        return total + jnp.dot(
            headw[:, chunk(i)], one_hot(i * CHUNK, CHUNK), preferred_element_type=F32
        )

    picked = lax.fori_loop(0, WHOLE, pick, jnp.zeros((CD, NW), F32))
    picked = picked + jnp.dot(
        headw[:, WHOLE * CHUNK:], one_hot(WHOLE * CHUNK, REST), preferred_element_type=F32
    )
    colw[mine] = picked.astype(BF16)
    pcol = go(remote(colw.at[mine], colw.at[mine], psend.at[1], precv.at[1], s, pc))
    tracks = jnp.broadcast_to(track[...].astype(F32), (8, NW))
    across = jnp.transpose(tracks)[:, :1]
    counts = jnp.sum((across == tracks[:1]).astype(F32), axis=0, keepdims=True)
    row = lax.broadcasted_iota(jnp.int32, (NL, NL), 0)
    col = lax.broadcasted_iota(jnp.int32, (NL, NL), 1)
    target = 4 * (col % 128) + col // 128
    target = jnp.where(q == 0, target, NL - 1 - target)
    order = (row == target).astype(F32).astype(BF16)
    lax.fori_loop(1, NS, gwait, 0)
    bases = gen[...].reshape(T, 128)
    hot = jnp.concatenate([(bases == n).astype(F32).astype(BF16) for n in range(4)], axis=1)
    letters[...] = nt(hot, order).astype(BF16)

    local[0].wait()
    pstem.wait_recv()
    state = nt(stemw[...], letters[...])

    def share(l):
        return go(remote(act.at[l], act2.at[l], a2send.at[l], a2recv.at[l], s, pc))

    for l in range(LAYERS):
        d = STEPS[l]
        sq = state * state
        th = jnp.tanh(ROOT * state * (1.0 + CUBE * sq))
        half = 0.5 * (1.0 + th)
        a = (state * half).astype(BF16)
        act[l, x, 0] = a[:CD]
        act[l, x, 1] = a[CD:]

        def ring(slot, h, j, n):
            return go(remote(
                act.at[l, slot, h], act.at[l, slot, h], asend.at[l, n], arecv.at[l, n], s, x_at(j)
            ))

        f0 = ring(x, 0, 1, 0)
        b1 = ring(x, 1, 3, 1)
        der[l] = half + (0.5 * ROOT) * state * (1.0 - th * th) * (1.0 + (3 * CUBE) * sq)
        lead(f0)
        f1 = ring(x, 1, 1, 2)
        lead(b1)
        b0 = ring(x, 0, 3, 3)
        f0.wait_recv()
        fr = ring((x + 3) % NX, 0, 1, 4)
        b1.wait_recv()
        br_ = ring((x + 1) % NX, 1, 3, 5)
        for k in range(3):
            local[2 + 3 * l + k].wait()
            pw[l][k].wait_recv()
        f1.wait_recv()
        b0.wait_recv()
        fr.wait_recv()
        br_.wait_recv()
        p = jnp.dot(
            wst[l].reshape(3 * CX, C), act[l].reshape(C, T), preferred_element_type=F32
        )
        state = (
            state + p[CX:2 * CX] + from_low(p[:CX], d) + from_high(p[2 * CX:], d)
        )

    bins = NS * lax.broadcasted_iota(jnp.int32, (T, NW), 0) + s
    begin = start[...]
    member = ((bins >= begin) & (bins < begin + WIN)).astype(F32)
    pooled = jnp.dot(state, member, precision=HIGH, preferred_element_type=F32) / WIN
    pcol.wait_recv()
    columns = colw[...].astype(F32)
    sone[c] = 0.5 * jnp.sum(pooled * columns, axis=0, keepdims=True)

    def one(j):
        to = (c + j) % NC
        return remote(sone.at[c], sone.at[c], ssone.at[j], rsone.at[j], s, to)

    ones = [go(one(j)) for j in range(1, NC)]

    def reduce_y(r, value):
        for i in range(2):
            for j in range(NY):
                rys[r, i, j] = value[CD * i:CD * (i + 1), 128 * j:128 * (j + 1)].astype(BF16)
        return [
            go(remote(
                rys.at[r, (q + i) % 2, (y + j) % NY], ryr.at[r, NY * i + j],
                r_ys.at[r, NY * i + j], r_yr.at[r, NY * i + j], y_at(j), 2 * x + (q + i) % 2,
            ))
            for j in range(NY) for i in range(2) if i + j > 0
        ]

    def reduce_z(r, copies):
        for copy in copies:
            copy.wait_recv()
        total = rys[r, q, y].astype(F32)
        for i in range(1, 2 * NY):
            total = total + ryr[r, i].astype(F32)
        rzb[r, z] = total.astype(BF16)
        return [
            go(remote(rzb.at[r, z], rzb.at[r, z], r_zs.at[r, j], r_zr.at[r, j], z_at(j), c))
            for j in range(1, NZ)
        ]

    def reduce_g(r, copies):
        for copy in copies:
            copy.wait_recv()
        total = rzb[r, 0].astype(F32)
        for j in range(1, NZ):
            total = total + rzb[r, j].astype(F32)
        rgb[r, y] = total
        return [
            go(remote(rgb.at[r, y], rgb.at[r, y], r_gs.at[r, j], r_gr.at[r, j], y_at(j), c))
            for j in range(1, NY)
        ]

    def reduce_end(r, copies):
        for copy in copies:
            copy.wait_recv()
        return jnp.concatenate([rgb[r, j] for j in range(NY)], axis=1)

    for copy in ones:
        copy.wait_recv()
    total = sone[0]
    for j in range(1, NC):
        total = total + sone[j]
    stwo[s] = total

    def two(j):
        to = (s + j) % NS
        return remote(stwo.at[s], stwo.at[s], sstwo.at[j], rstwo.at[j], to, c)

    def two_start(j, _):
        two(j).start()
        return 0

    def two_wait(j, _):
        two(j).wait_recv()
        return 0

    def two_done(j, _):
        two(j).wait_send()
        return 0

    lax.fori_loop(1, NS, two_start, 0)
    pool_copies = reduce_y(0, pooled)
    a2 = {4: share(4), 3: share(3)}
    lax.fori_loop(1, NS, two_wait, 0)
    score = stwo[0]
    for j in range(1, NS):
        score = score + stwo[j]
    score_out[...] = score
    slope = (jnp.exp(score) - targets[...]) / counts
    grad = nt((0.5 / WIN) * slope * columns, member, precision=HIGH)

    waiting_y = None
    waiting_z = []

    def y_stage(item):
        l, copies = item
        for copy in copies:
            copy.wait_recv()
        own = pl.ds(pl.multiple_of(CX * y, CX), CX)
        total = wg[l, own].astype(F32)
        for j in range(1, NY):
            total = total + yrecv[l, j].astype(F32)
        total = total.reshape(NZ, CZ, KO)
        zacc[l] = total
        zsend[l] = total.astype(BF16)
        sends = [
            go(remote(
                zsend.at[l, (z + j) % NZ], zrecv.at[l, j], zs.at[l, j], zr.at[l, j], z_at(j), c
            ))
            for j in range(1, NZ)
        ]
        waiting_z.append((l, sends))

    def z_stage(item):
        l, copies = item
        for copy in copies:
            copy.wait_recv()
        total = zacc[l, z]
        for j in range(1, NZ):
            total = total + zrecv[l, j].astype(F32)
        for k in range(3):
            conv_out[l, k] = total[:, CD * k:CD * (k + 1)]

    def place(first, last):
        def body(i, _):
            head_out[:, chunk(i)] = spread_out(one_hot(i * CHUNK, CHUNK))
            return 0

        lax.fori_loop(first, last, body, 0)

    def spread_out(hot):
        out = nt(thirds[...], hot)
        return out[:CD] + out[CD:2 * CD] + out[2 * CD:]

    for l in reversed(range(LAYERS)):
        d = STEPS[l]
        u = grad.astype(BF16)
        up[l] = u
        ucopy = go(remote(up.at[l, other], upx.at[l], us.at[l], ur.at[l], s, pc))
        u = u.astype(F32)
        taps = jnp.concatenate(
            [from_high(u, d).astype(BF16), u.astype(BF16), from_low(u, d).astype(BF16)], axis=0
        )
        p = tn(wst[l].reshape(3 * CX, C), taps)
        part[...] = p
        for i in range(NX):
            for h in range(2):
                at = CX * i + CD * h
                bsend[l, i, h] = p[at:at + CD].astype(BF16)

        def shed(src, n, j):
            return go(remote(src, brecv.at[l, n], bs.at[l, n], br.at[l, n], s, x_at(j)))

        far = (x + 2) % NX
        right = (x + 1) % NX
        left = (x + 3) % NX
        f1 = shed(bsend.at[l, far, 1], 0, 1)
        b0 = shed(bsend.at[l, far, 0], 1, 3)
        if l >= 2:
            a2[l - 2] = share(l - 2)
        first = q == 0
        v = up[l, mine].astype(F32)
        vh, vl = from_high(v, d).astype(BF16), from_low(v, d).astype(BF16)
        own_taps = jnp.concatenate(
            [jnp.where(first, vh, vl), v.astype(BF16), jnp.where(first, vl, vh)], axis=0
        )
        g = nt(act[l].reshape(C, T), own_taps)
        lead(f1)
        f0 = shed(bsend.at[l, right, 0], 2, 1)
        lead(b0)
        b1 = shed(bsend.at[l, left, 1], 3, 3)
        ucopy.wait_recv()
        a2[l].wait_recv()
        w = upx[l].astype(F32)
        wh, wl = from_high(w, d).astype(BF16), from_low(w, d).astype(BF16)
        far_taps = jnp.concatenate(
            [jnp.where(first, wl, wh), w.astype(BF16), jnp.where(first, wh, wl)], axis=0
        )
        wg[l] = (g + nt(act2[l].reshape(C, T), far_taps)).astype(BF16)
        ysends = [
            go(remote(
                wg.at[l, pl.ds(pl.multiple_of(CX * ((y + j) % NY), CX), CX)], yrecv.at[l, j],
                ys.at[l, j], yr.at[l, j], y_at(j), c,
            ))
            for j in range(1, NY)
        ]
        f1.wait_recv()
        b0.wait_recv()
        at = pl.ds(pl.multiple_of(CX * right + CD, CD), CD)
        bcomb[l, 0] = (part[at] + brecv[l, 0].astype(F32)).astype(BF16)
        fc = shed(bcomb.at[l, 0], 4, 1)
        at = pl.ds(pl.multiple_of(CX * left, CD), CD)
        bcomb[l, 1] = (part[at] + brecv[l, 1].astype(F32)).astype(BF16)
        bc = shed(bcomb.at[l, 1], 5, 3)
        if waiting_y is not None:
            y_stage(waiting_y)
        waiting_y = (l, ysends)
        if len(waiting_z) > 1:
            z_stage(waiting_z.pop(0))
        if l == LAYERS - 1:
            pool_copies = reduce_z(0, pool_copies)
        if l == LAYERS - 2:
            pool_copies = reduce_g(0, pool_copies)
        if l == LAYERS - 3:
            terms = 0.5 * slope * reduce_end(0, pool_copies)
            for i in range(3):
                piece = terms.astype(BF16)
                thirds[CD * i:CD * (i + 1)] = piece
                terms = terms - piece.astype(F32)
            place(0, WHOLE // 2)
        if l == LAYERS - 4:
            place(WHOLE // 2, WHOLE)
            head_out[:, WHOLE * CHUNK:] = spread_out(one_hot(WHOLE * CHUNK, REST))
        f0.wait_recv()
        b1.wait_recv()
        fc.wait_recv()
        bc.wait_recv()
        own0 = part[pl.ds(pl.multiple_of(CX * x, CD), CD)]
        own1 = part[pl.ds(pl.multiple_of(CX * x + CD, CD), CD)]
        low = own0 + brecv[l, 2].astype(F32) + brecv[l, 5].astype(F32)
        high = own1 + brecv[l, 3].astype(F32) + brecv[l, 4].astype(F32)
        grad = grad + jnp.concatenate([low, high], axis=0) * der[l]

    stem_copies = reduce_y(
        1, jnp.dot(grad.astype(BF16), letters[...], preferred_element_type=F32)
    )
    y_stage(waiting_y)
    z_stage(waiting_z.pop(0))
    stem_copies = reduce_z(1, stem_copies)
    while waiting_z:
        z_stage(waiting_z.pop(0))
    stem_copies = reduce_g(1, stem_copies)
    stem_out[...] = reduce_end(1, stem_copies)

    lax.fori_loop(1, NS, gdone, 0)
    lax.fori_loop(1, NS, two_done, 0)
    for copy in pending:
        copy.wait_send()


def deliver(score, conv, stem, head, score_to, conv_to, stem_to, head_to, sem):
    copies = [
        pltpu.make_async_copy(
            head.at[pl.ds(24 * i, 24)], head_to.at[pl.ds(24 * i, 24)], sem.at[2 + LAYERS + i]
        )
        for i in range(4)
    ]
    for l in range(LAYERS):
        copies.append(pltpu.make_async_copy(conv.at[l], conv_to.at[l], sem.at[2 + l]))
    copies.append(pltpu.make_async_copy(stem, stem_to, sem.at[0]))
    copies.append(pltpu.make_async_copy(score, score_to, sem.at[1]))
    for copy in copies:
        copy.start()
    for copy in copies:
        copy.wait()


def shards(
    genome, stem_weight, dilated_filter_weight, head_weight, window_start, window_track, targets
):
    dma = pltpu.SemaphoreType.DMA
    V = pltpu.VMEM
    scratch = [
        V((NS, T // NS, 128), jnp.int32), V((NS, T // NS, 128), jnp.int32), dma((NS,)), dma((NS,)),
        V((CD, TRACKS), BF16),
        V((CX, NL), BF16), V((CX, NW), BF16), V((LAYERS, 3, CX, C), BF16),
        dma((17,)), dma((17,)), dma((17,)),
        V((T, NL), BF16),
        V((LAYERS, NX, 2, CD, T), BF16), V((LAYERS, NX, 2, CD, T), BF16),
        V((LAYERS, CX, T), F32), dma((LAYERS, 6)), dma((LAYERS, 6)),
        dma((LAYERS,)), dma((LAYERS,)),
        V((NC, 1, NW), F32), dma((NC,)), dma((NC,)),
        V((NS, 1, NW), F32), dma((NS,)), dma((NS,)),
        V((C, T), F32), V((LAYERS, NX, 2, CD, T), BF16), V((LAYERS, 6, CD, T), BF16),
        V((LAYERS, 2, CD, T), BF16), dma((LAYERS, 6)), dma((LAYERS, 6)),
        V((LAYERS, CX, T), BF16), V((LAYERS, CD, T), BF16), dma((LAYERS,)), dma((LAYERS,)),
        V((LAYERS, C, KO), BF16), V((LAYERS, NY, CX, KO), BF16),
        dma((LAYERS, NY)), dma((LAYERS, NY)),
        V((LAYERS, NZ, CZ, KO), F32), V((LAYERS, NZ, CZ, KO), BF16),
        V((LAYERS, NZ, CZ, KO), BF16), dma((LAYERS, NZ)), dma((LAYERS, NZ)),
        V((2, 2, NY, CD, 128), BF16), V((2, 2 * NY, CD, 128), BF16),
        V((2, NZ, CD, 128), BF16), V((2, NY, CD, 128), F32),
        dma((2, 2 * NY)), dma((2, 2 * NY)), dma((2, NZ)), dma((2, NZ)),
        dma((2, NY)), dma((2, NY)), V((KO, NW), BF16),
    ]
    vm = pl.BlockSpec(memory_space=pltpu.VMEM)
    hbm = pl.BlockSpec(memory_space=pl.ANY)
    score, conv_grad, stem_grad, head_grad = pl.pallas_call(
        tower,
        out_shape=(
            V((1, NW), F32), V((LAYERS, 3, CZ, CD), F32), V((CD, NL), F32), V((CD, TRACKS), F32),
        ),
        in_specs=[vm, hbm, hbm, hbm, vm, vm, vm],
        out_specs=(vm, vm, vm, vm),
        scratch_shapes=scratch,
        compiler_params=pltpu.CompilerParams(
            collective_id=0, has_side_effects=True, vmem_limit_bytes=60 * 1024 * 1024
        ),
    )(
        genome, stem_weight, dilated_filter_weight, head_weight,
        window_start.reshape(1, NW), window_track.reshape(1, NW), targets.reshape(1, NW),
    )
    results = (score, conv_grad, stem_grad, head_grad)
    score, conv_grad, stem_grad, head_grad = pl.pallas_call(
        deliver,
        out_shape=tuple(jax.ShapeDtypeStruct(r.shape, F32) for r in results),
        in_specs=[vm] * 4,
        out_specs=(hbm,) * 4,
        scratch_shapes=[dma((2 + LAYERS + 4,))],
    )(*[pltpu.with_memory_space_constraint(r, pltpu.VMEM) for r in results])
    return (score.reshape(NW), conv_grad.transpose(0, 1, 3, 2), stem_grad, head_grad)


def solution(mesh):
    return jax.shard_map(
        shards,
        mesh=mesh,
        in_specs=(
            P("seq", None),
            P("ch", None),
            P(None, None, "ch", None),
            P("ch", None),
            P(),
            P(),
            P(),
        ),
        out_specs=(P(), P(None, None, "ch", "seq"), P("ch", None), P("ch", None)),
        check_vma=False,
    )
```

```python
import functools

import jax
import jax.numpy as jnp
from jax import lax
from jax.experimental import pallas as pl
from jax.experimental.pallas import tpu as pltpu
from jax.sharding import PartitionSpec as P

LAYERS = 5
WIN = 16
STEPS = (1, 4, 8, 16, 32)
MESH = pl.DeviceIdType.MESH
F32 = jnp.float32
BF16 = jnp.bfloat16
HIGH = lax.Precision.HIGHEST
NX, NY, NZ, NS, NC = 4, 4, 8, 32, 8
T = 256
C = 768
CX = 192
CD = 96
NW = 512
NL = 512
KO = 3 * CD
CZ = 24
TRACKS = 5313
CHUNK = 512
WHOLE = TRACKS // CHUNK
REST = TRACKS - WHOLE * CHUNK
ROOT = 0.7978845608028654
CUBE = 0.044715


def nt(a, b, **kw):
    return lax.dot_general(a, b, (((1,), (1,)), ((), ())), preferred_element_type=F32, **kw)


def tn(a, b):
    return lax.dot_general(a, b, (((0,), (0,)), ((), ())), preferred_element_type=F32)


def from_low(v, d):
    lane = lax.broadcasted_iota(jnp.int32, v.shape, 1)
    return jnp.where(lane >= d, pltpu.roll(v, d, 1), 0.0)


def from_high(v, d):
    lane = lax.broadcasted_iota(jnp.int32, v.shape, 1)
    return jnp.where(lane < v.shape[1] - d, pltpu.roll(v, v.shape[1] - d, 1), 0.0)


def tower(
    genome, stem, weight, head, start, track, targets,
    score_to, conv_to, stem_to, head_to,
    score_out, conv_out, stem_out, head_out, out_sem,
    gbuf, gen, gsend, grecv, headw,
    stemw, colw, wst, local_sem, psend, precv,
    letters, act, act2, der, asend, arecv, a2send, a2recv,
    sone, ssone, rsone, stwo, sstwo, rstwo,
    part, bsend, brecv, bcomb, bs, br,
    up, upx, us, ur,
    wg, yrecv, ys, yr, zacc, zsend, zrecv, zs, zr,
    rys, ryr, rzb, rgb, r_ys, r_yr, r_zs, r_zr, r_gs, r_gr, thirds,
):
    s = lax.axis_index("seq")
    c = lax.axis_index("ch")
    y = s // NZ
    z = s % NZ
    x = c // 2
    q = c % 2
    pc = 2 * x + (1 - q)
    pending = []
    leaving = []

    def leave(src, dst, n):
        copy = pltpu.make_async_copy(src, dst, out_sem.at[n])
        copy.start()
        leaving.append(copy)

    def one_hot(base, width):
        ids = lax.broadcasted_iota(jnp.int32, (width, NW), 0) + base
        return (ids == track[...]).astype(F32).astype(BF16)

    def chunk(i):
        return pl.ds(pl.multiple_of(i * CHUNK, CHUNK), CHUNK)

    def remote(src, dst, ssem, rsem, seq, ch):
        return pltpu.make_async_remote_copy(
            src_ref=src, dst_ref=dst, send_sem=ssem, recv_sem=rsem,
            device_id=(seq, ch), device_id_type=MESH,
        )

    def go(copy):
        copy.start()
        pending.append(copy)
        return copy

    def lead(copy):
        pending[:] = [p for p in pending if p is not copy]
        copy.wait_send()

    def x_at(j):
        return 2 * ((x + j) % NX) + q

    def y_at(j):
        return ((y + j) % NY) * NZ + z

    def z_at(j):
        return y * NZ + (z + j) % NZ

    mine = pl.ds(pl.multiple_of(CD * q, CD), CD)
    other = pl.ds(pl.multiple_of(CD * (1 - q), CD), CD)

    local = [
        pltpu.make_async_copy(stem, stemw.at[mine], local_sem.at[0]),
        pltpu.make_async_copy(head, headw, local_sem.at[1]),
    ]
    for l in range(LAYERS):
        for k in range(3):
            local.append(
                pltpu.make_async_copy(
                    weight.at[l, k], wst.at[l, k + q * (2 - 2 * k), mine],
                    local_sem.at[2 + 3 * l + k],
                )
            )
    for copy in local:
        copy.start()

    barrier = pltpu.get_barrier_semaphore()

    def greet_seq(j, _):
        pl.semaphore_signal(barrier, inc=1, device_id=((s + j) % NS, c), device_id_type=MESH)
        return 0

    def greet_ch(j, _):
        pl.semaphore_signal(barrier, inc=1, device_id=(s, (c + j) % NC), device_id_type=MESH)
        return 0

    lax.fori_loop(1, NS, greet_seq, 0)
    lax.fori_loop(1, NC, greet_ch, 0)
    for j in range(1, NY):
        pl.semaphore_signal(barrier, inc=1, device_id=(y_at(j), pc), device_id_type=MESH)
    for r in range(NS):
        gbuf[r] = genome[pl.ds(r, T // NS, stride=NS), :]
    pl.semaphore_wait(barrier, NS - 1 + NC - 1 + NY - 1)

    def gcopy(j):
        to = (s + j) % NS
        return remote(gbuf.at[to], gen.at[s], gsend.at[j], grecv.at[j], to, c)

    def gstart(j, _):
        gcopy(j).start()
        return 0

    def gwait(j, _):
        gcopy(j).wait_recv()
        return 0

    def gdone(j, _):
        gcopy(j).wait_send()
        return 0

    lax.fori_loop(1, NS, gstart, 0)
    pstem = go(remote(stem, stemw.at[mine], psend.at[0], precv.at[0], s, pc))
    pw = []
    for l in range(LAYERS):
        pw.append([
            go(remote(
                weight.at[l, k], wst.at[l, k + (1 - q) * (2 - 2 * k), mine],
                psend.at[2 + 3 * l + k], precv.at[2 + 3 * l + k], s, pc,
            ))
            for k in range(3)
        ])

    gen[s] = gbuf[s]
    local[1].wait()

    def pick(i, total):
        return total + jnp.dot(
            headw[:, chunk(i)], one_hot(i * CHUNK, CHUNK), preferred_element_type=F32
        )

    picked = lax.fori_loop(0, WHOLE, pick, jnp.zeros((CD, NW), F32))
    picked = picked + jnp.dot(
        headw[:, WHOLE * CHUNK:], one_hot(WHOLE * CHUNK, REST), preferred_element_type=F32
    )
    colw[mine] = picked.astype(BF16)
    pcol = go(remote(colw.at[mine], colw.at[mine], psend.at[1], precv.at[1], s, pc))
    tracks = jnp.broadcast_to(track[...].astype(F32), (8, NW))
    across = jnp.transpose(tracks)[:, :1]
    counts = jnp.sum((across == tracks[:1]).astype(F32), axis=0, keepdims=True)
    row = lax.broadcasted_iota(jnp.int32, (NL, NL), 0)
    col = lax.broadcasted_iota(jnp.int32, (NL, NL), 1)
    target = 4 * (col % 128) + col // 128
    target = jnp.where(q == 0, target, NL - 1 - target)
    order = (row == target).astype(F32).astype(BF16)
    lax.fori_loop(1, NS, gwait, 0)
    bases = gen[...].reshape(T, 128)
    hot = jnp.concatenate([(bases == n).astype(F32).astype(BF16) for n in range(4)], axis=1)
    letters[...] = nt(hot, order).astype(BF16)

    local[0].wait()
    pstem.wait_recv()
    state = nt(stemw[...], letters[...])

    def share(l):
        return go(remote(act.at[l], act2.at[l], a2send.at[l], a2recv.at[l], s, pc))

    for l in range(LAYERS):
        d = STEPS[l]
        sq = state * state
        th = jnp.tanh(ROOT * state * (1.0 + CUBE * sq))
        half = 0.5 * (1.0 + th)
        a = (state * half).astype(BF16)
        act[l, x, 0] = a[:CD]
        act[l, x, 1] = a[CD:]

        def ring(slot, h, j, n):
            return go(remote(
                act.at[l, slot, h], act.at[l, slot, h], asend.at[l, n], arecv.at[l, n], s, x_at(j)
            ))

        f0 = ring(x, 0, 1, 0)
        b1 = ring(x, 1, 3, 1)
        der[l] = half + (0.5 * ROOT) * state * (1.0 - th * th) * (1.0 + (3 * CUBE) * sq)
        lead(f0)
        f1 = ring(x, 1, 1, 2)
        lead(b1)
        b0 = ring(x, 0, 3, 3)
        f0.wait_recv()
        fr = ring((x + 3) % NX, 0, 1, 4)
        b1.wait_recv()
        br_ = ring((x + 1) % NX, 1, 3, 5)
        for k in range(3):
            local[2 + 3 * l + k].wait()
            pw[l][k].wait_recv()
        f1.wait_recv()
        b0.wait_recv()
        fr.wait_recv()
        br_.wait_recv()
        p = jnp.dot(
            wst[l].reshape(3 * CX, C), act[l].reshape(C, T), preferred_element_type=F32
        )
        state = (
            state + p[CX:2 * CX] + from_low(p[:CX], d) + from_high(p[2 * CX:], d)
        )

    bins = NS * lax.broadcasted_iota(jnp.int32, (T, NW), 0) + s
    begin = start[...]
    member = ((bins >= begin) & (bins < begin + WIN)).astype(F32)
    pooled = jnp.dot(state, member, precision=HIGH, preferred_element_type=F32) / WIN
    pcol.wait_recv()
    columns = colw[...].astype(F32)
    sone[c] = 0.5 * jnp.sum(pooled * columns, axis=0, keepdims=True)

    def one(j):
        to = (c + j) % NC
        return remote(sone.at[c], sone.at[c], ssone.at[j], rsone.at[j], s, to)

    ones = [go(one(j)) for j in range(1, NC)]

    def reduce_y(r, value):
        for i in range(2):
            for j in range(NY):
                rys[r, i, j] = value[CD * i:CD * (i + 1), 128 * j:128 * (j + 1)].astype(BF16)
        return [
            go(remote(
                rys.at[r, (q + i) % 2, (y + j) % NY], ryr.at[r, NY * i + j],
                r_ys.at[r, NY * i + j], r_yr.at[r, NY * i + j], y_at(j), 2 * x + (q + i) % 2,
            ))
            for j in range(NY) for i in range(2) if i + j > 0
        ]

    def reduce_z(r, copies):
        for copy in copies:
            copy.wait_recv()
        total = rys[r, q, y].astype(F32)
        for i in range(1, 2 * NY):
            total = total + ryr[r, i].astype(F32)
        rzb[r, z] = total.astype(BF16)
        return [
            go(remote(rzb.at[r, z], rzb.at[r, z], r_zs.at[r, j], r_zr.at[r, j], z_at(j), c))
            for j in range(1, NZ)
        ]

    def reduce_g(r, copies):
        for copy in copies:
            copy.wait_recv()
        total = rzb[r, 0].astype(F32)
        for j in range(1, NZ):
            total = total + rzb[r, j].astype(F32)
        rgb[r, y] = total
        return [
            go(remote(rgb.at[r, y], rgb.at[r, y], r_gs.at[r, j], r_gr.at[r, j], y_at(j), c))
            for j in range(1, NY)
        ]

    def reduce_end(r, copies):
        for copy in copies:
            copy.wait_recv()
        return jnp.concatenate([rgb[r, j] for j in range(NY)], axis=1)

    for copy in ones:
        copy.wait_recv()
    total = sone[0]
    for j in range(1, NC):
        total = total + sone[j]
    stwo[s] = total

    def two(j):
        to = (s + j) % NS
        return remote(stwo.at[s], stwo.at[s], sstwo.at[j], rstwo.at[j], to, c)

    def two_start(j, _):
        two(j).start()
        return 0

    def two_wait(j, _):
        two(j).wait_recv()
        return 0

    def two_done(j, _):
        two(j).wait_send()
        return 0

    lax.fori_loop(1, NS, two_start, 0)
    pool_copies = reduce_y(0, pooled)
    a2 = {4: share(4), 3: share(3)}
    lax.fori_loop(1, NS, two_wait, 0)
    score = stwo[0]
    for j in range(1, NS):
        score = score + stwo[j]
    score_out[...] = score
    leave(score_out, score_to, LAYERS)
    slope = (jnp.exp(score) - targets[...]) / counts
    grad = nt((0.5 / WIN) * slope * columns, member, precision=HIGH)

    waiting_y = None
    waiting_z = []

    def y_stage(item):
        l, copies = item
        for copy in copies:
            copy.wait_recv()
        own = pl.ds(pl.multiple_of(CX * y, CX), CX)
        total = wg[l, own].astype(F32)
        for j in range(1, NY):
            total = total + yrecv[l, j].astype(F32)
        total = total.reshape(NZ, CZ, KO)
        zacc[l] = total
        zsend[l] = total.astype(BF16)
        sends = [
            go(remote(
                zsend.at[l, (z + j) % NZ], zrecv.at[l, j], zs.at[l, j], zr.at[l, j], z_at(j), c
            ))
            for j in range(1, NZ)
        ]
        waiting_z.append((l, sends))

    def z_stage(item):
        l, copies = item
        for copy in copies:
            copy.wait_recv()
        total = zacc[l, z]
        for j in range(1, NZ):
            total = total + zrecv[l, j].astype(F32)
        for k in range(3):
            conv_out[l, k] = total[:, CD * k:CD * (k + 1)]
        leave(conv_out.at[l], conv_to.at[l], l)

    def place(first, last):
        def body(i, _):
            head_out[:, chunk(i)] = spread_out(one_hot(i * CHUNK, CHUNK))
            return 0

        lax.fori_loop(first, last, body, 0)

    def spread_out(hot):
        out = nt(thirds[...], hot)
        return out[:CD] + out[CD:2 * CD] + out[2 * CD:]

    for l in reversed(range(LAYERS)):
        d = STEPS[l]
        u = grad.astype(BF16)
        up[l] = u
        ucopy = go(remote(up.at[l, other], upx.at[l], us.at[l], ur.at[l], s, pc))
        u = u.astype(F32)
        taps = jnp.concatenate(
            [from_high(u, d).astype(BF16), u.astype(BF16), from_low(u, d).astype(BF16)], axis=0
        )
        p = tn(wst[l].reshape(3 * CX, C), taps)
        part[...] = p
        for i in range(NX):
            for h in range(2):
                at = CX * i + CD * h
                bsend[l, i, h] = p[at:at + CD].astype(BF16)

        def shed(src, n, j):
            return go(remote(src, brecv.at[l, n], bs.at[l, n], br.at[l, n], s, x_at(j)))

        far = (x + 2) % NX
        right = (x + 1) % NX
        left = (x + 3) % NX
        f1 = shed(bsend.at[l, far, 1], 0, 1)
        b0 = shed(bsend.at[l, far, 0], 1, 3)
        if l >= 2:
            a2[l - 2] = share(l - 2)
        first = q == 0
        v = up[l, mine].astype(F32)
        vh, vl = from_high(v, d).astype(BF16), from_low(v, d).astype(BF16)
        own_taps = jnp.concatenate(
            [jnp.where(first, vh, vl), v.astype(BF16), jnp.where(first, vl, vh)], axis=0
        )
        g = nt(act[l].reshape(C, T), own_taps)
        lead(f1)
        f0 = shed(bsend.at[l, right, 0], 2, 1)
        lead(b0)
        b1 = shed(bsend.at[l, left, 1], 3, 3)
        ucopy.wait_recv()
        a2[l].wait_recv()
        w = upx[l].astype(F32)
        wh, wl = from_high(w, d).astype(BF16), from_low(w, d).astype(BF16)
        far_taps = jnp.concatenate(
            [jnp.where(first, wl, wh), w.astype(BF16), jnp.where(first, wh, wl)], axis=0
        )
        wg[l] = (g + nt(act2[l].reshape(C, T), far_taps)).astype(BF16)
        ysends = [
            go(remote(
                wg.at[l, pl.ds(pl.multiple_of(CX * ((y + j) % NY), CX), CX)], yrecv.at[l, j],
                ys.at[l, j], yr.at[l, j], y_at(j), c,
            ))
            for j in range(1, NY)
        ]
        f1.wait_recv()
        b0.wait_recv()
        at = pl.ds(pl.multiple_of(CX * right + CD, CD), CD)
        bcomb[l, 0] = (part[at] + brecv[l, 0].astype(F32)).astype(BF16)
        fc = shed(bcomb.at[l, 0], 4, 1)
        at = pl.ds(pl.multiple_of(CX * left, CD), CD)
        bcomb[l, 1] = (part[at] + brecv[l, 1].astype(F32)).astype(BF16)
        bc = shed(bcomb.at[l, 1], 5, 3)
        if waiting_y is not None:
            y_stage(waiting_y)
        waiting_y = (l, ysends)
        if len(waiting_z) > 1:
            z_stage(waiting_z.pop(0))
        if l == LAYERS - 1:
            pool_copies = reduce_z(0, pool_copies)
        if l == LAYERS - 2:
            pool_copies = reduce_g(0, pool_copies)
        if l == LAYERS - 3:
            terms = 0.5 * slope * reduce_end(0, pool_copies)
            for i in range(3):
                piece = terms.astype(BF16)
                thirds[CD * i:CD * (i + 1)] = piece
                terms = terms - piece.astype(F32)
            place(0, WHOLE // 2)
        if l == LAYERS - 4:
            place(WHOLE // 2, WHOLE)
            head_out[:, WHOLE * CHUNK:] = spread_out(one_hot(WHOLE * CHUNK, REST))
            leave(head_out, head_to, LAYERS + 1)
        f0.wait_recv()
        b1.wait_recv()
        fc.wait_recv()
        bc.wait_recv()
        own0 = part[pl.ds(pl.multiple_of(CX * x, CD), CD)]
        own1 = part[pl.ds(pl.multiple_of(CX * x + CD, CD), CD)]
        low = own0 + brecv[l, 2].astype(F32) + brecv[l, 5].astype(F32)
        high = own1 + brecv[l, 3].astype(F32) + brecv[l, 4].astype(F32)
        grad = grad + jnp.concatenate([low, high], axis=0) * der[l]

    stem_copies = reduce_y(
        1, jnp.dot(grad.astype(BF16), letters[...], preferred_element_type=F32)
    )
    y_stage(waiting_y)
    z_stage(waiting_z.pop(0))
    stem_copies = reduce_z(1, stem_copies)
    while waiting_z:
        z_stage(waiting_z.pop(0))
    stem_copies = reduce_g(1, stem_copies)
    stem_out[...] = reduce_end(1, stem_copies)
    leave(stem_out, stem_to, LAYERS + 2)

    lax.fori_loop(1, NS, gdone, 0)
    lax.fori_loop(1, NS, two_done, 0)
    for copy in pending:
        copy.wait_send()
    for copy in leaving:
        copy.wait()


def deliver(score, conv, stem, head, score_to, conv_to, stem_to, head_to, sem):
    copies = [
        pltpu.make_async_copy(
            head.at[pl.ds(24 * i, 24)], head_to.at[pl.ds(24 * i, 24)], sem.at[2 + LAYERS + i]
        )
        for i in range(4)
    ]
    for l in range(LAYERS):
        copies.append(pltpu.make_async_copy(conv.at[l], conv_to.at[l], sem.at[2 + l]))
    copies.append(pltpu.make_async_copy(stem, stem_to, sem.at[0]))
    copies.append(pltpu.make_async_copy(score, score_to, sem.at[1]))
    for copy in copies:
        copy.start()
    for copy in copies:
        copy.wait()


def shards(
    genome, stem_weight, dilated_filter_weight, head_weight, window_start, window_track, targets
):
    dma = pltpu.SemaphoreType.DMA
    V = pltpu.VMEM
    results = [
        V((1, NW), F32), V((LAYERS, 3, CZ, CD), F32), V((CD, NL), F32), V((CD, TRACKS), F32),
    ]
    scratch = results + [
        dma((LAYERS + 3,)),
        V((NS, T // NS, 128), jnp.int32), V((NS, T // NS, 128), jnp.int32), dma((NS,)), dma((NS,)),
        V((CD, TRACKS), BF16),
        V((CX, NL), BF16), V((CX, NW), BF16), V((LAYERS, 3, CX, C), BF16),
        dma((17,)), dma((17,)), dma((17,)),
        V((T, NL), BF16),
        V((LAYERS, NX, 2, CD, T), BF16), V((LAYERS, NX, 2, CD, T), BF16),
        V((LAYERS, CX, T), F32), dma((LAYERS, 6)), dma((LAYERS, 6)),
        dma((LAYERS,)), dma((LAYERS,)),
        V((NC, 1, NW), F32), dma((NC,)), dma((NC,)),
        V((NS, 1, NW), F32), dma((NS,)), dma((NS,)),
        V((C, T), F32), V((LAYERS, NX, 2, CD, T), BF16), V((LAYERS, 6, CD, T), BF16),
        V((LAYERS, 2, CD, T), BF16), dma((LAYERS, 6)), dma((LAYERS, 6)),
        V((LAYERS, CX, T), BF16), V((LAYERS, CD, T), BF16), dma((LAYERS,)), dma((LAYERS,)),
        V((LAYERS, C, KO), BF16), V((LAYERS, NY, CX, KO), BF16),
        dma((LAYERS, NY)), dma((LAYERS, NY)),
        V((LAYERS, NZ, CZ, KO), F32), V((LAYERS, NZ, CZ, KO), BF16),
        V((LAYERS, NZ, CZ, KO), BF16), dma((LAYERS, NZ)), dma((LAYERS, NZ)),
        V((2, 2, NY, CD, 128), BF16), V((2, 2 * NY, CD, 128), BF16),
        V((2, NZ, CD, 128), BF16), V((2, NY, CD, 128), F32),
        dma((2, 2 * NY)), dma((2, 2 * NY)), dma((2, NZ)), dma((2, NZ)),
        dma((2, NY)), dma((2, NY)), V((KO, NW), BF16),
    ]
    vm = pl.BlockSpec(memory_space=pltpu.VMEM)
    hbm = pl.BlockSpec(memory_space=pl.ANY)
    score, conv_grad, stem_grad, head_grad = pl.pallas_call(
        tower,
        out_shape=tuple(results),
        in_specs=[vm, hbm, hbm, hbm, vm, vm, vm],
        out_specs=(hbm, hbm, hbm, hbm),
        scratch_shapes=scratch,
        compiler_params=pltpu.CompilerParams(
            collective_id=0, has_side_effects=True, vmem_limit_bytes=60 * 1024 * 1024
        ),
    )(
        genome, stem_weight, dilated_filter_weight, head_weight,
        window_start.reshape(1, NW), window_track.reshape(1, NW), targets.reshape(1, NW),
    )
    results = (score, conv_grad, stem_grad, head_grad)
    score, conv_grad, stem_grad, head_grad = pl.pallas_call(
        deliver,
        out_shape=tuple(jax.ShapeDtypeStruct(r.shape, F32) for r in results),
        in_specs=[vm] * 4,
        out_specs=(hbm,) * 4,
        scratch_shapes=[dma((2 + LAYERS + 4,))],
    )(*[pltpu.with_memory_space_constraint(r, pltpu.VMEM) for r in results])
    return (score.reshape(NW), conv_grad.transpose(0, 1, 3, 2), stem_grad, head_grad)


def solution(mesh):
    return jax.shard_map(
        shards,
        mesh=mesh,
        in_specs=(
            P("seq", None),
            P("ch", None),
            P(None, None, "ch", None),
            P("ch", None),
            P(),
            P(),
            P(),
        ),
        out_specs=(P(), P(None, None, "ch", "seq"), P("ch", None), P("ch", None)),
        check_vma=False,
    )
```

```python
import functools

import jax
import jax.numpy as jnp
from jax import lax
from jax.experimental import pallas as pl
from jax.experimental.pallas import tpu as pltpu
from jax.sharding import PartitionSpec as P

LAYERS = 5
WIN = 16
STEPS = (1, 4, 8, 16, 32)
MESH = pl.DeviceIdType.MESH
F32 = jnp.float32
BF16 = jnp.bfloat16
HIGH = lax.Precision.HIGHEST
NX, NY, NZ, NS, NC = 4, 4, 8, 32, 8
T = 256
C = 768
CX = 192
CD = 96
NW = 512
NL = 512
KO = 3 * CD
CZ = 24
TRACKS = 5313
CHUNK = 512
WHOLE = TRACKS // CHUNK
REST = TRACKS - WHOLE * CHUNK
ROOT = 0.7978845608028654
CUBE = 0.044715


def nt(a, b, **kw):
    return lax.dot_general(a, b, (((1,), (1,)), ((), ())), preferred_element_type=F32, **kw)


def tn(a, b):
    return lax.dot_general(a, b, (((0,), (0,)), ((), ())), preferred_element_type=F32)


def from_low(v, d):
    lane = lax.broadcasted_iota(jnp.int32, v.shape, 1)
    return jnp.where(lane >= d, pltpu.roll(v, d, 1), 0.0)


def from_high(v, d):
    lane = lax.broadcasted_iota(jnp.int32, v.shape, 1)
    return jnp.where(lane < v.shape[1] - d, pltpu.roll(v, v.shape[1] - d, 1), 0.0)


def tower(
    genome, stem, weight, head, start, track, targets,
    score_out, conv_out, stem_out, head_out,
    gbuf, gen, gsend, grecv, headw,
    stemw, colw, wst, local_sem, psend, precv,
    letters, act, act2, der, asend, arecv, a2send, a2recv,
    sone, ssone, rsone, stwo, sstwo, rstwo,
    part, bsend, brecv, bcomb, bs, br,
    up, upx, us, ur,
    wg, yrecv, ys, yr, zacc, zsend, zrecv, zs, zr,
    rys, ryr, rzb, rgb, r_ys, r_yr, r_zs, r_zr, r_gs, r_gr, thirds,
):
    s = lax.axis_index("seq")
    c = lax.axis_index("ch")
    y = s // NZ
    z = s % NZ
    x = c // 2
    q = c % 2
    pc = 2 * x + (1 - q)
    pending = []

    def one_hot(base, width):
        ids = lax.broadcasted_iota(jnp.int32, (width, NW), 0) + base
        return (ids == track[...]).astype(F32).astype(BF16)

    def chunk(i):
        return pl.ds(pl.multiple_of(i * CHUNK, CHUNK), CHUNK)

    def remote(src, dst, ssem, rsem, seq, ch):
        return pltpu.make_async_remote_copy(
            src_ref=src, dst_ref=dst, send_sem=ssem, recv_sem=rsem,
            device_id=(seq, ch), device_id_type=MESH,
        )

    def go(copy):
        copy.start()
        pending.append(copy)
        return copy

    def fire(copy):
        copy.start()
        return copy

    def all_of(ref, sem):
        pltpu.make_async_copy(ref, ref, sem).wait()

    ending = []

    def x_at(j):
        return 2 * ((x + j) % NX) + q

    def y_at(j):
        return ((y + j) % NY) * NZ + z

    def z_at(j):
        return y * NZ + (z + j) % NZ

    mine = pl.ds(pl.multiple_of(CD * q, CD), CD)
    other = pl.ds(pl.multiple_of(CD * (1 - q), CD), CD)

    local = [
        pltpu.make_async_copy(stem, stemw.at[mine], local_sem.at[0]),
        pltpu.make_async_copy(head, headw, local_sem.at[1]),
    ]
    for l in range(LAYERS):
        for k in range(3):
            local.append(
                pltpu.make_async_copy(
                    weight.at[l, k], wst.at[l, k + q * (2 - 2 * k), mine],
                    local_sem.at[2 + l],
                )
            )
    for copy in local:
        copy.start()

    barrier = pltpu.get_barrier_semaphore()

    def greet_seq(j, _):
        pl.semaphore_signal(barrier, inc=1, device_id=((s + j) % NS, c), device_id_type=MESH)
        return 0

    def greet_ch(j, _):
        pl.semaphore_signal(barrier, inc=1, device_id=(s, (c + j) % NC), device_id_type=MESH)
        return 0

    lax.fori_loop(1, NS, greet_seq, 0)
    lax.fori_loop(1, NC, greet_ch, 0)
    for j in range(1, NY):
        pl.semaphore_signal(barrier, inc=1, device_id=(y_at(j), pc), device_id_type=MESH)
    for r in range(NS):
        gbuf[r] = genome[pl.ds(r, T // NS, stride=NS), :]
    pl.semaphore_wait(barrier, NS - 1 + NC - 1 + NY - 1)

    def gcopy(j):
        to = (s + j) % NS
        return remote(gbuf.at[to], gen.at[s], gsend.at[0], grecv.at[0], to, c)

    def gstart(j, _):
        gcopy(j).start()
        return 0

    lax.fori_loop(1, NS, gstart, 0)
    pstem = go(remote(stem, stemw.at[mine], psend.at[0], precv.at[0], s, pc))
    pw = []
    for l in range(LAYERS):
        pw.append([
            fire(remote(
                weight.at[l, k], wst.at[l, k + (1 - q) * (2 - 2 * k), mine],
                psend.at[2 + l], precv.at[2 + l], s, pc,
            ))
            for k in range(3)
        ])
        ending.append((wst.at[l, :, mine], psend.at[2 + l]))

    gen[s] = gbuf[s]
    local[1].wait()

    def pick(i, total):
        return total + jnp.dot(
            headw[:, chunk(i)], one_hot(i * CHUNK, CHUNK), preferred_element_type=F32
        )

    picked = lax.fori_loop(0, WHOLE, pick, jnp.zeros((CD, NW), F32))
    picked = picked + jnp.dot(
        headw[:, WHOLE * CHUNK:], one_hot(WHOLE * CHUNK, REST), preferred_element_type=F32
    )
    colw[mine] = picked.astype(BF16)
    pcol = go(remote(colw.at[mine], colw.at[mine], psend.at[1], precv.at[1], s, pc))
    tracks = jnp.broadcast_to(track[...].astype(F32), (8, NW))
    across = jnp.transpose(tracks)[:, :1]
    counts = jnp.sum((across == tracks[:1]).astype(F32), axis=0, keepdims=True)
    row = lax.broadcasted_iota(jnp.int32, (NL, NL), 0)
    col = lax.broadcasted_iota(jnp.int32, (NL, NL), 1)
    target = 4 * (col % 128) + col // 128
    target = jnp.where(q == 0, target, NL - 1 - target)
    order = (row == target).astype(F32).astype(BF16)
    all_of(gen.at[pl.ds(0, NS - 1)], grecv.at[0])
    bases = gen[...].reshape(T, 128)
    hot = jnp.concatenate([(bases == n).astype(F32).astype(BF16) for n in range(4)], axis=1)
    letters[...] = nt(hot, order).astype(BF16)

    local[0].wait()
    pstem.wait_recv()
    state = nt(stemw[...], letters[...])

    def share(l):
        return go(remote(act.at[l], act2.at[l], a2send.at[l], a2recv.at[l], s, pc))

    for l in range(LAYERS):
        d = STEPS[l]
        sq = state * state
        th = jnp.tanh(ROOT * state * (1.0 + CUBE * sq))
        half = 0.5 * (1.0 + th)
        a = (state * half).astype(BF16)
        act[l, x, 0] = a[:CD]
        act[l, x, 1] = a[CD:]

        def ring(slot, h, j, n):
            return fire(remote(
                act.at[l, slot, h], act.at[l, slot, h], asend.at[l], arecv.at[l, min(n, 2)],
                s, x_at(j),
            ))

        f0 = ring(x, 0, 1, 0)
        b1 = ring(x, 1, 3, 1)
        der[l] = half + (0.5 * ROOT) * state * (1.0 - th * th) * (1.0 + (3 * CUBE) * sq)
        ring(x, 1, 1, 2)
        ring(x, 0, 3, 3)
        f0.wait_recv()
        ring((x + 3) % NX, 0, 1, 4)
        b1.wait_recv()
        ring((x + 1) % NX, 1, 3, 5)
        all_of(wst.at[l, :, mine], local_sem.at[2 + l])
        all_of(wst.at[l, :, mine], precv.at[2 + l])
        all_of(act.at[l, pl.ds(0, 2)], arecv.at[l, 2])
        ending.append((act.at[l, pl.ds(0, 3)], asend.at[l]))
        p = jnp.dot(
            wst[l].reshape(3 * CX, C), act[l].reshape(C, T), preferred_element_type=F32
        )
        state = (
            state + p[CX:2 * CX] + from_low(p[:CX], d) + from_high(p[2 * CX:], d)
        )

    bins = NS * lax.broadcasted_iota(jnp.int32, (T, NW), 0) + s
    begin = start[...]
    member = ((bins >= begin) & (bins < begin + WIN)).astype(F32)
    pooled = jnp.dot(state, member, precision=HIGH, preferred_element_type=F32) / WIN
    pcol.wait_recv()
    columns = colw[...].astype(F32)
    sone[c] = 0.5 * jnp.sum(pooled * columns, axis=0, keepdims=True)

    def one(j):
        to = (c + j) % NC
        return remote(sone.at[c], sone.at[c], ssone.at[0], rsone.at[0], s, to)

    for j in range(1, NC):
        one(j).start()
    ending.append((sone.at[pl.ds(0, NC - 1)], ssone.at[0]))

    def reduce_y(r, value):
        for i in range(2):
            for j in range(NY):
                rys[r, i, j] = value[CD * i:CD * (i + 1), 128 * j:128 * (j + 1)].astype(BF16)
        return [
            fire(remote(
                rys.at[r, (q + i) % 2, (y + j) % NY], ryr.at[r, NY * i + j],
                r_ys.at[r], r_yr.at[r], y_at(j), 2 * x + (q + i) % 2,
            ))
            for j in range(NY) for i in range(2) if i + j > 0
        ]

    def reduce_z(r, copies):
        all_of(ryr.at[r, pl.ds(1, 2 * NY - 1)], r_yr.at[r])
        ending.append((ryr.at[r, pl.ds(1, 2 * NY - 1)], r_ys.at[r]))
        total = rys[r, q, y].astype(F32)
        for i in range(1, 2 * NY):
            total = total + ryr[r, i].astype(F32)
        rzb[r, z] = total.astype(BF16)
        return [
            fire(remote(rzb.at[r, z], rzb.at[r, z], r_zs.at[r], r_zr.at[r], z_at(j), c))
            for j in range(1, NZ)
        ]

    def reduce_g(r, copies):
        all_of(rzb.at[r, pl.ds(1, NZ - 1)], r_zr.at[r])
        ending.append((rzb.at[r, pl.ds(1, NZ - 1)], r_zs.at[r]))
        total = rzb[r, 0].astype(F32)
        for j in range(1, NZ):
            total = total + rzb[r, j].astype(F32)
        rgb[r, y] = total
        return [
            fire(remote(rgb.at[r, y], rgb.at[r, y], r_gs.at[r], r_gr.at[r], y_at(j), c))
            for j in range(1, NY)
        ]

    def reduce_end(r, copies):
        all_of(rgb.at[r, pl.ds(1, NY - 1)], r_gr.at[r])
        ending.append((rgb.at[r, pl.ds(1, NY - 1)], r_gs.at[r]))
        return jnp.concatenate([rgb[r, j] for j in range(NY)], axis=1)

    all_of(sone.at[pl.ds(0, NC - 1)], rsone.at[0])
    total = sone[0]
    for j in range(1, NC):
        total = total + sone[j]
    stwo[s] = total

    def two(j):
        to = (s + j) % NS
        return remote(stwo.at[s], stwo.at[s], sstwo.at[0], rstwo.at[0], to, c)

    def two_start(j, _):
        two(j).start()
        return 0

    lax.fori_loop(1, NS, two_start, 0)
    pool_copies = reduce_y(0, pooled)
    a2 = {4: share(4), 3: share(3)}
    all_of(stwo.at[pl.ds(0, NS - 1)], rstwo.at[0])
    score = stwo[0]
    for j in range(1, NS):
        score = score + stwo[j]
    score_out[...] = score
    slope = (jnp.exp(score) - targets[...]) / counts
    grad = nt((0.5 / WIN) * slope * columns, member, precision=HIGH)

    waiting_y = None
    waiting_z = []

    def y_stage(item):
        l, copies = item
        all_of(yrecv.at[l, pl.ds(1, NY - 1)], yr.at[l])
        ending.append((yrecv.at[l, pl.ds(1, NY - 1)], ys.at[l]))
        own = pl.ds(pl.multiple_of(CX * y, CX), CX)
        total = wg[l, own].astype(F32)
        for j in range(1, NY):
            total = total + yrecv[l, j].astype(F32)
        total = total.reshape(NZ, CZ, KO)
        zacc[l] = total
        zsend[l] = total.astype(BF16)
        sends = [
            fire(remote(
                zsend.at[l, (z + j) % NZ], zrecv.at[l, j], zs.at[l], zr.at[l], z_at(j), c
            ))
            for j in range(1, NZ)
        ]
        waiting_z.append((l, sends))

    def z_stage(item):
        l, copies = item
        all_of(zrecv.at[l, pl.ds(1, NZ - 1)], zr.at[l])
        ending.append((zrecv.at[l, pl.ds(1, NZ - 1)], zs.at[l]))
        total = zacc[l, z]
        for j in range(1, NZ):
            total = total + zrecv[l, j].astype(F32)
        for k in range(3):
            conv_out[l, k] = total[:, CD * k:CD * (k + 1)]

    def place(first, last):
        def body(i, _):
            head_out[:, chunk(i)] = spread_out(one_hot(i * CHUNK, CHUNK))
            return 0

        lax.fori_loop(first, last, body, 0)

    def spread_out(hot):
        out = nt(thirds[...], hot)
        return out[:CD] + out[CD:2 * CD] + out[2 * CD:]

    for l in reversed(range(LAYERS)):
        d = STEPS[l]
        u = grad.astype(BF16)
        up[l] = u
        ucopy = go(remote(up.at[l, other], upx.at[l], us.at[l], ur.at[l], s, pc))
        u = u.astype(F32)
        taps = jnp.concatenate(
            [from_high(u, d).astype(BF16), u.astype(BF16), from_low(u, d).astype(BF16)], axis=0
        )
        p = tn(wst[l].reshape(3 * CX, C), taps)
        part[...] = p
        for i in range(NX):
            for h in range(2):
                at = CX * i + CD * h
                bsend[l, i, h] = p[at:at + CD].astype(BF16)

        def shed(src, n, j):
            return fire(remote(
                src, brecv.at[l, n], bs.at[l], br.at[l, min(n, 2)], s, x_at(j)
            ))

        far = (x + 2) % NX
        right = (x + 1) % NX
        left = (x + 3) % NX
        f1 = shed(bsend.at[l, far, 1], 0, 1)
        b0 = shed(bsend.at[l, far, 0], 1, 3)
        if l >= 2:
            a2[l - 2] = share(l - 2)
        first = q == 0
        v = up[l, mine].astype(F32)
        vh, vl = from_high(v, d).astype(BF16), from_low(v, d).astype(BF16)
        own_taps = jnp.concatenate(
            [jnp.where(first, vh, vl), v.astype(BF16), jnp.where(first, vl, vh)], axis=0
        )
        g = nt(act[l].reshape(C, T), own_taps)
        shed(bsend.at[l, right, 0], 2, 1)
        shed(bsend.at[l, left, 1], 3, 3)
        ucopy.wait_recv()
        a2[l].wait_recv()
        w = upx[l].astype(F32)
        wh, wl = from_high(w, d).astype(BF16), from_low(w, d).astype(BF16)
        far_taps = jnp.concatenate(
            [jnp.where(first, wl, wh), w.astype(BF16), jnp.where(first, wh, wl)], axis=0
        )
        wg[l] = (g + nt(act2[l].reshape(C, T), far_taps)).astype(BF16)
        ysends = [
            fire(remote(
                wg.at[l, pl.ds(pl.multiple_of(CX * ((y + j) % NY), CX), CX)], yrecv.at[l, j],
                ys.at[l], yr.at[l], y_at(j), c,
            ))
            for j in range(1, NY)
        ]
        f1.wait_recv()
        b0.wait_recv()
        at = pl.ds(pl.multiple_of(CX * right + CD, CD), CD)
        bcomb[l, 0] = (part[at] + brecv[l, 0].astype(F32)).astype(BF16)
        shed(bcomb.at[l, 0], 4, 1)
        at = pl.ds(pl.multiple_of(CX * left, CD), CD)
        bcomb[l, 1] = (part[at] + brecv[l, 1].astype(F32)).astype(BF16)
        shed(bcomb.at[l, 1], 5, 3)
        if waiting_y is not None:
            y_stage(waiting_y)
        waiting_y = (l, ysends)
        if len(waiting_z) > 1:
            z_stage(waiting_z.pop(0))
        if l == LAYERS - 1:
            pool_copies = reduce_z(0, pool_copies)
        if l == LAYERS - 2:
            pool_copies = reduce_g(0, pool_copies)
        if l == LAYERS - 3:
            terms = 0.5 * slope * reduce_end(0, pool_copies)
            for i in range(3):
                piece = terms.astype(BF16)
                thirds[CD * i:CD * (i + 1)] = piece
                terms = terms - piece.astype(F32)
            place(0, WHOLE // 2)
        if l == LAYERS - 4:
            place(WHOLE // 2, WHOLE)
            head_out[:, WHOLE * CHUNK:] = spread_out(one_hot(WHOLE * CHUNK, REST))
        all_of(brecv.at[l, pl.ds(2, 4)], br.at[l, 2])
        ending.append((brecv.at[l], bs.at[l]))
        own0 = part[pl.ds(pl.multiple_of(CX * x, CD), CD)]
        own1 = part[pl.ds(pl.multiple_of(CX * x + CD, CD), CD)]
        low = own0 + brecv[l, 2].astype(F32) + brecv[l, 5].astype(F32)
        high = own1 + brecv[l, 3].astype(F32) + brecv[l, 4].astype(F32)
        grad = grad + jnp.concatenate([low, high], axis=0) * der[l]

    stem_copies = reduce_y(
        1, jnp.dot(grad.astype(BF16), letters[...], preferred_element_type=F32)
    )
    y_stage(waiting_y)
    z_stage(waiting_z.pop(0))
    stem_copies = reduce_z(1, stem_copies)
    while waiting_z:
        z_stage(waiting_z.pop(0))
    stem_copies = reduce_g(1, stem_copies)
    stem_out[...] = reduce_end(1, stem_copies)

    all_of(gen.at[pl.ds(0, NS - 1)], gsend.at[0])
    all_of(stwo.at[pl.ds(0, NS - 1)], sstwo.at[0])
    for ref, sem in ending:
        all_of(ref, sem)
    for copy in pending:
        copy.wait_send()


def deliver(score, conv, stem, head, score_to, conv_to, stem_to, head_to, sem):
    copies = [
        pltpu.make_async_copy(
            head.at[pl.ds(24 * i, 24)], head_to.at[pl.ds(24 * i, 24)], sem.at[2 + LAYERS + i]
        )
        for i in range(4)
    ]
    for l in range(LAYERS):
        copies.append(pltpu.make_async_copy(conv.at[l], conv_to.at[l], sem.at[2 + l]))
    copies.append(pltpu.make_async_copy(stem, stem_to, sem.at[0]))
    copies.append(pltpu.make_async_copy(score, score_to, sem.at[1]))
    for copy in copies:
        copy.start()
    for copy in copies:
        copy.wait()


def shards(
    genome, stem_weight, dilated_filter_weight, head_weight, window_start, window_track, targets
):
    dma = pltpu.SemaphoreType.DMA
    V = pltpu.VMEM
    scratch = [
        V((NS, T // NS, 128), jnp.int32), V((NS, T // NS, 128), jnp.int32), dma((1,)), dma((1,)),
        V((CD, TRACKS), BF16),
        V((CX, NL), BF16), V((CX, NW), BF16), V((LAYERS, 3, CX, C), BF16),
        dma((2 + LAYERS,)), dma((2 + LAYERS,)), dma((2 + LAYERS,)),
        V((T, NL), BF16),
        V((LAYERS, NX, 2, CD, T), BF16), V((LAYERS, NX, 2, CD, T), BF16),
        V((LAYERS, CX, T), F32), dma((LAYERS,)), dma((LAYERS, 3)),
        dma((LAYERS,)), dma((LAYERS,)),
        V((NC, 1, NW), F32), dma((1,)), dma((1,)),
        V((NS, 1, NW), F32), dma((1,)), dma((1,)),
        V((C, T), F32), V((LAYERS, NX, 2, CD, T), BF16), V((LAYERS, 6, CD, T), BF16),
        V((LAYERS, 2, CD, T), BF16), dma((LAYERS,)), dma((LAYERS, 3)),
        V((LAYERS, CX, T), BF16), V((LAYERS, CD, T), BF16), dma((LAYERS,)), dma((LAYERS,)),
        V((LAYERS, C, KO), BF16), V((LAYERS, NY, CX, KO), BF16),
        dma((LAYERS,)), dma((LAYERS,)),
        V((LAYERS, NZ, CZ, KO), F32), V((LAYERS, NZ, CZ, KO), BF16),
        V((LAYERS, NZ, CZ, KO), BF16), dma((LAYERS,)), dma((LAYERS,)),
        V((2, 2, NY, CD, 128), BF16), V((2, 2 * NY, CD, 128), BF16),
        V((2, NZ, CD, 128), BF16), V((2, NY, CD, 128), F32),
        dma((2,)), dma((2,)), dma((2,)), dma((2,)), dma((2,)), dma((2,)), V((KO, NW), BF16),
    ]
    vm = pl.BlockSpec(memory_space=pltpu.VMEM)
    hbm = pl.BlockSpec(memory_space=pl.ANY)
    score, conv_grad, stem_grad, head_grad = pl.pallas_call(
        tower,
        out_shape=(
            V((1, NW), F32), V((LAYERS, 3, CZ, CD), F32), V((CD, NL), F32), V((CD, TRACKS), F32),
        ),
        in_specs=[vm, hbm, hbm, hbm, vm, vm, vm],
        out_specs=(vm, vm, vm, vm),
        scratch_shapes=scratch,
        compiler_params=pltpu.CompilerParams(
            collective_id=0, has_side_effects=True, vmem_limit_bytes=60 * 1024 * 1024
        ),
    )(
        genome, stem_weight, dilated_filter_weight, head_weight,
        window_start.reshape(1, NW), window_track.reshape(1, NW), targets.reshape(1, NW),
    )
    results = (score, conv_grad, stem_grad, head_grad)
    score, conv_grad, stem_grad, head_grad = pl.pallas_call(
        deliver,
        out_shape=tuple(jax.ShapeDtypeStruct(r.shape, F32) for r in results),
        in_specs=[vm] * 4,
        out_specs=(hbm,) * 4,
        scratch_shapes=[dma((2 + LAYERS + 4,))],
    )(*[pltpu.with_memory_space_constraint(r, pltpu.VMEM) for r in results])
    return (score.reshape(NW), conv_grad.transpose(0, 1, 3, 2), stem_grad, head_grad)


def solution(mesh):
    return jax.shard_map(
        shards,
        mesh=mesh,
        in_specs=(
            P("seq", None),
            P("ch", None),
            P(None, None, "ch", None),
            P("ch", None),
            P(),
            P(),
            P(),
        ),
        out_specs=(P(), P(None, None, "ch", "seq"), P("ch", None), P("ch", None)),
        check_vma=False,
    )
```

```python
import functools

import jax
import jax.numpy as jnp
from jax import lax
from jax.experimental import pallas as pl
from jax.experimental.pallas import tpu as pltpu
from jax.sharding import PartitionSpec as P

LAYERS = 5
WIN = 16
STEPS = (1, 4, 8, 16, 32)
MESH = pl.DeviceIdType.MESH
F32 = jnp.float32
BF16 = jnp.bfloat16
HIGH = lax.Precision.HIGHEST
NX, NY, NZ, NS, NC = 4, 4, 8, 32, 8
T = 256
C = 768
CX = 192
CD = 96
NW = 512
NL = 512
KO = 3 * CD
CZ = 24
TRACKS = 5313
CHUNK = 512
WHOLE = TRACKS // CHUNK
REST = TRACKS - WHOLE * CHUNK
ROOT = 0.7978845608028654
CUBE = 0.044715


def nt(a, b, **kw):
    return lax.dot_general(a, b, (((1,), (1,)), ((), ())), preferred_element_type=F32, **kw)


def tn(a, b):
    return lax.dot_general(a, b, (((0,), (0,)), ((), ())), preferred_element_type=F32)


def from_low(v, d):
    lane = lax.broadcasted_iota(jnp.int32, v.shape, 1)
    return jnp.where(lane >= d, pltpu.roll(v, d, 1), 0.0)


def from_high(v, d):
    lane = lax.broadcasted_iota(jnp.int32, v.shape, 1)
    return jnp.where(lane < v.shape[1] - d, pltpu.roll(v, v.shape[1] - d, 1), 0.0)


def tower(
    genome, stem, weight, head, start, track, targets,
    score_out, conv_out, stem_out, head_out,
    gbuf, gen, gsend, grecv, headw,
    stemw, colw, wst, local_sem, psend, precv,
    letters, act, act2, der, asend, arecv, a2send, a2recv,
    sone, ssone, rsone, stwo, sstwo, rstwo,
    part, bsend, brecv, bcomb, bs, br,
    up, upx, us, ur,
    wg, yrecv, ys, yr, zacc, zsend, zrecv, zs, zr,
    rys, ryr, rzb, rgb, r_ys, r_yr, r_zs, r_zr, r_gs, r_gr, thirds,
):
    s = lax.axis_index("seq")
    c = lax.axis_index("ch")
    y = s // NZ
    z = s % NZ
    x = c // 2
    q = c % 2
    pc = 2 * x + (1 - q)
    pending = []

    def one_hot(base, width):
        ids = lax.broadcasted_iota(jnp.int32, (width, NW), 0) + base
        return (ids == track[...]).astype(F32).astype(BF16)

    def chunk(i):
        return pl.ds(pl.multiple_of(i * CHUNK, CHUNK), CHUNK)

    def remote(src, dst, ssem, rsem, seq, ch):
        return pltpu.make_async_remote_copy(
            src_ref=src, dst_ref=dst, send_sem=ssem, recv_sem=rsem,
            device_id=(seq, ch), device_id_type=MESH,
        )

    def go(copy):
        copy.start()
        pending.append(copy)
        return copy

    def fire(copy):
        copy.start()
        return copy

    def all_of(ref, sem):
        pltpu.make_async_copy(ref, ref, sem).wait()

    ending = []

    def x_at(j):
        return 2 * ((x + j) % NX) + q

    def y_at(j):
        return ((y + j) % NY) * NZ + z

    def z_at(j):
        return y * NZ + (z + j) % NZ

    mine = pl.ds(pl.multiple_of(CD * q, CD), CD)
    other = pl.ds(pl.multiple_of(CD * (1 - q), CD), CD)

    local = [
        pltpu.make_async_copy(stem, stemw.at[mine], local_sem.at[0]),
        pltpu.make_async_copy(head, headw, local_sem.at[1]),
    ]
    for l in range(LAYERS):
        for k in range(3):
            local.append(
                pltpu.make_async_copy(
                    weight.at[l, k], wst.at[l, k + q * (2 - 2 * k), mine],
                    local_sem.at[2 + l],
                )
            )
    for copy in local:
        copy.start()

    barrier = pltpu.get_barrier_semaphore()

    def greet_seq(j, _):
        pl.semaphore_signal(barrier, inc=1, device_id=((s + j) % NS, c), device_id_type=MESH)
        return 0

    def greet_ch(j, _):
        pl.semaphore_signal(barrier, inc=1, device_id=(s, (c + j) % NC), device_id_type=MESH)
        return 0

    lax.fori_loop(1, NS, greet_seq, 0)
    lax.fori_loop(1, NC, greet_ch, 0)
    for j in range(1, NY):
        pl.semaphore_signal(barrier, inc=1, device_id=(y_at(j), pc), device_id_type=MESH)
    for r in range(NS):
        gbuf[r] = genome[pl.ds(r, T // NS, stride=NS), :]
    pl.semaphore_wait(barrier, NS - 1 + NC - 1 + NY - 1)

    def gcopy(j):
        to = (s + j) % NS
        return remote(gbuf.at[to], gen.at[s], gsend.at[0], grecv.at[0], to, c)

    def gstart(j, _):
        gcopy(j).start()
        return 0

    lax.fori_loop(1, NS, gstart, 0)
    pstem = go(remote(stem, stemw.at[mine], psend.at[0], precv.at[0], s, pc))
    pw = []
    for l in range(LAYERS):
        pw.append([
            fire(remote(
                weight.at[l, k], wst.at[l, k + (1 - q) * (2 - 2 * k), mine],
                psend.at[2 + l], precv.at[2 + l], s, pc,
            ))
            for k in range(3)
        ])
        ending.append((wst.at[l, :, mine], psend.at[2 + l]))

    gen[s] = gbuf[s]
    local[1].wait()

    def pick(i, total):
        return total + jnp.dot(
            headw[:, chunk(i)], one_hot(i * CHUNK, CHUNK), preferred_element_type=F32
        )

    picked = lax.fori_loop(0, WHOLE, pick, jnp.zeros((CD, NW), F32))
    picked = picked + jnp.dot(
        headw[:, WHOLE * CHUNK:], one_hot(WHOLE * CHUNK, REST), preferred_element_type=F32
    )
    colw[mine] = picked.astype(BF16)
    pcol = go(remote(colw.at[mine], colw.at[mine], psend.at[1], precv.at[1], s, pc))
    tracks = jnp.broadcast_to(track[...].astype(F32), (8, NW))
    across = jnp.transpose(tracks)[:, :1]
    counts = jnp.sum((across == tracks[:1]).astype(F32), axis=0, keepdims=True)
    row = lax.broadcasted_iota(jnp.int32, (NL, NL), 0)
    col = lax.broadcasted_iota(jnp.int32, (NL, NL), 1)
    target = 4 * (col % 128) + col // 128
    target = jnp.where(q == 0, target, NL - 1 - target)
    order = (row == target).astype(F32).astype(BF16)
    all_of(gen.at[pl.ds(0, NS - 1)], grecv.at[0])
    bases = gen[...].reshape(T, 128)
    hot = jnp.concatenate([(bases == n).astype(F32).astype(BF16) for n in range(4)], axis=1)
    letters[...] = nt(hot, order).astype(BF16)

    local[0].wait()
    pstem.wait_recv()
    state = nt(stemw[...], letters[...])

    def share(l):
        return go(remote(act.at[l], act2.at[l], a2send.at[l], a2recv.at[l], s, pc))

    for l in range(LAYERS):
        d = STEPS[l]
        sq = state * state
        th = jnp.tanh(ROOT * state * (1.0 + CUBE * sq))
        half = 0.5 * (1.0 + th)
        a = (state * half).astype(BF16)
        act[l, x, 0] = a[:CD]
        act[l, x, 1] = a[CD:]

        def ring(slot, h, j, n):
            return fire(remote(
                act.at[l, slot, h], act.at[l, slot, h], asend.at[l], arecv.at[l, min(n, 2)],
                s, x_at(j),
            ))

        f0 = ring(x, 0, 1, 0)
        b1 = ring(x, 1, 3, 1)
        der[l] = half + (0.5 * ROOT) * state * (1.0 - th * th) * (1.0 + (3 * CUBE) * sq)
        ring(x, 1, 1, 2)
        ring(x, 0, 3, 3)
        f0.wait_recv()
        ring((x + 3) % NX, 0, 1, 4)
        b1.wait_recv()
        ring((x + 1) % NX, 1, 3, 5)
        all_of(wst.at[l, :, mine], local_sem.at[2 + l])
        all_of(wst.at[l, :, mine], precv.at[2 + l])
        all_of(act.at[l, pl.ds(0, 2)], arecv.at[l, 2])
        ending.append((act.at[l, pl.ds(0, 3)], asend.at[l]))
        p = jnp.dot(
            wst[l].reshape(3 * CX, C), act[l].reshape(C, T), preferred_element_type=F32
        )
        state = (
            state + p[CX:2 * CX] + from_low(p[:CX], d) + from_high(p[2 * CX:], d)
        )

    bins = NS * lax.broadcasted_iota(jnp.int32, (T, NW), 0) + s
    begin = start[...]
    member = ((bins >= begin) & (bins < begin + WIN)).astype(F32)
    pooled = jnp.dot(state, member, precision=HIGH, preferred_element_type=F32) / WIN
    pcol.wait_recv()
    columns = colw[...].astype(F32)
    sone[c] = 0.5 * jnp.sum(pooled * columns, axis=0, keepdims=True)

    def one(j):
        to = (c + j) % NC
        return remote(sone.at[c], sone.at[c], ssone.at[0], rsone.at[0], s, to)

    for j in range(1, NC):
        one(j).start()
    ending.append((sone.at[pl.ds(0, NC - 1)], ssone.at[0]))

    def reduce_y(r, value):
        for i in range(2):
            for j in range(NY):
                rys[r, i, j] = value[CD * i:CD * (i + 1), 128 * j:128 * (j + 1)].astype(BF16)
        return [
            fire(remote(
                rys.at[r, (q + i) % 2, (y + j) % NY], ryr.at[r, NY * i + j],
                r_ys.at[r], r_yr.at[r], y_at(j), 2 * x + (q + i) % 2,
            ))
            for j in range(NY) for i in range(2) if i + j > 0
        ]

    def reduce_z(r, copies):
        all_of(ryr.at[r, pl.ds(1, 2 * NY - 1)], r_yr.at[r])
        ending.append((ryr.at[r, pl.ds(1, 2 * NY - 1)], r_ys.at[r]))
        total = rys[r, q, y].astype(F32)
        for i in range(1, 2 * NY):
            total = total + ryr[r, i].astype(F32)
        rzb[r, z] = total.astype(BF16)
        return [
            fire(remote(rzb.at[r, z], rzb.at[r, z], r_zs.at[r], r_zr.at[r], z_at(j), c))
            for j in range(1, NZ)
        ]

    def reduce_g(r, copies):
        all_of(rzb.at[r, pl.ds(1, NZ - 1)], r_zr.at[r])
        ending.append((rzb.at[r, pl.ds(1, NZ - 1)], r_zs.at[r]))
        total = rzb[r, 0].astype(F32)
        for j in range(1, NZ):
            total = total + rzb[r, j].astype(F32)
        rgb[r, y] = total
        return [
            fire(remote(rgb.at[r, y], rgb.at[r, y], r_gs.at[r], r_gr.at[r], y_at(j), c))
            for j in range(1, NY)
        ]

    def reduce_end(r, copies):
        all_of(rgb.at[r, pl.ds(1, NY - 1)], r_gr.at[r])
        ending.append((rgb.at[r, pl.ds(1, NY - 1)], r_gs.at[r]))
        return jnp.concatenate([rgb[r, j] for j in range(NY)], axis=1)

    all_of(sone.at[pl.ds(0, NC - 1)], rsone.at[0])
    total = sone[0]
    for j in range(1, NC):
        total = total + sone[j]
    stwo[s] = total

    def two(j):
        to = (s + j) % NS
        return remote(stwo.at[s], stwo.at[s], sstwo.at[0], rstwo.at[0], to, c)

    def two_start(j, _):
        two(j).start()
        return 0

    lax.fori_loop(1, NS, two_start, 0)
    pool_copies = reduce_y(0, pooled)
    a2 = {4: share(4), 3: share(3)}
    all_of(stwo.at[pl.ds(0, NS - 1)], rstwo.at[0])
    score = stwo[0]
    for j in range(1, NS):
        score = score + stwo[j]
    score_out[...] = score
    slope = (jnp.exp(score) - targets[...]) / counts
    grad = nt((0.5 / WIN) * slope * columns, member, precision=HIGH)

    waiting_y = None
    waiting_z = []

    def y_stage(item):
        l, copies = item
        all_of(yrecv.at[l, pl.ds(1, NY - 1)], yr.at[l])
        ending.append((yrecv.at[l, pl.ds(1, NY - 1)], ys.at[l]))
        own = pl.ds(pl.multiple_of(CX * y, CX), CX)
        total = wg[l, own].astype(F32)
        for j in range(1, NY):
            total = total + yrecv[l, j].astype(F32)
        total = total.reshape(NZ, CZ, KO)
        zacc[l] = total
        zsend[l] = total.astype(BF16)
        sends = [
            fire(remote(
                zsend.at[l, (z + j) % NZ], zrecv.at[l, j], zs.at[l], zr.at[l], z_at(j), c
            ))
            for j in range(1, NZ)
        ]
        waiting_z.append((l, sends))

    def z_stage(item):
        l, copies = item
        all_of(zrecv.at[l, pl.ds(1, NZ - 1)], zr.at[l])
        ending.append((zrecv.at[l, pl.ds(1, NZ - 1)], zs.at[l]))
        total = zacc[l, z]
        for j in range(1, NZ):
            total = total + zrecv[l, j].astype(F32)
        for k in range(3):
            conv_out[l, k] = total[:, CD * k:CD * (k + 1)]

    def place(first, last):
        def body(i, _):
            head_out[:, chunk(i)] = spread_out(one_hot(i * CHUNK, CHUNK))
            return 0

        lax.fori_loop(first, last, body, 0)

    def spread_out(hot):
        out = nt(thirds[...], hot)
        return out[:CD] + out[CD:2 * CD] + out[2 * CD:]

    for l in reversed(range(LAYERS)):
        d = STEPS[l]
        u = grad.astype(BF16)
        up[l] = u
        ucopy = go(remote(up.at[l, other], upx.at[l], us.at[l], ur.at[l], s, pc))
        u = u.astype(F32)
        taps = jnp.concatenate(
            [from_high(u, d).astype(BF16), u.astype(BF16), from_low(u, d).astype(BF16)], axis=0
        )
        p = tn(wst[l].reshape(3 * CX, C), taps)
        part[...] = p
        for i in range(NX):
            for h in range(2):
                at = CX * i + CD * h
                bsend[l, i, h] = p[at:at + CD].astype(BF16)

        def shed(src, n, j):
            return fire(remote(
                src, brecv.at[l, n], bs.at[l], br.at[l, min(n, 2)], s, x_at(j)
            ))

        far = (x + 2) % NX
        right = (x + 1) % NX
        left = (x + 3) % NX
        f1 = shed(bsend.at[l, far, 1], 0, 1)
        b0 = shed(bsend.at[l, far, 0], 1, 3)
        if l >= 2:
            a2[l - 2] = share(l - 2)
        first = q == 0
        v = up[l, mine].astype(F32)
        vh, vl = from_high(v, d).astype(BF16), from_low(v, d).astype(BF16)
        own_taps = jnp.concatenate(
            [jnp.where(first, vh, vl), v.astype(BF16), jnp.where(first, vl, vh)], axis=0
        )
        g = nt(act[l].reshape(C, T), own_taps)
        shed(bsend.at[l, right, 0], 2, 1)
        shed(bsend.at[l, left, 1], 3, 3)
        ucopy.wait_recv()
        a2[l].wait_recv()
        w = upx[l].astype(F32)
        wh, wl = from_high(w, d).astype(BF16), from_low(w, d).astype(BF16)
        far_taps = jnp.concatenate(
            [jnp.where(first, wl, wh), w.astype(BF16), jnp.where(first, wh, wl)], axis=0
        )
        wg[l] = (g + nt(act2[l].reshape(C, T), far_taps)).astype(BF16)
        ysends = [
            fire(remote(
                wg.at[l, pl.ds(pl.multiple_of(CX * ((y + j) % NY), CX), CX)], yrecv.at[l, j],
                ys.at[l], yr.at[l], y_at(j), c,
            ))
            for j in range(1, NY)
        ]
        f1.wait_recv()
        b0.wait_recv()
        at = pl.ds(pl.multiple_of(CX * right + CD, CD), CD)
        bcomb[l, 0] = (part[at] + brecv[l, 0].astype(F32)).astype(BF16)
        shed(bcomb.at[l, 0], 4, 1)
        at = pl.ds(pl.multiple_of(CX * left, CD), CD)
        bcomb[l, 1] = (part[at] + brecv[l, 1].astype(F32)).astype(BF16)
        shed(bcomb.at[l, 1], 5, 3)
        if waiting_y is not None:
            y_stage(waiting_y)
        waiting_y = (l, ysends)
        if len(waiting_z) > 1:
            z_stage(waiting_z.pop(0))
        if l == LAYERS - 1:
            pool_copies = reduce_z(0, pool_copies)
        if l == LAYERS - 2:
            pool_copies = reduce_g(0, pool_copies)
        if l == LAYERS - 3:
            terms = 0.5 * slope * reduce_end(0, pool_copies)
            for i in range(3):
                piece = terms.astype(BF16)
                thirds[CD * i:CD * (i + 1)] = piece
                terms = terms - piece.astype(F32)
            place(0, WHOLE // 2)
        if l == LAYERS - 4:
            place(WHOLE // 2, WHOLE)
            head_out[:, WHOLE * CHUNK:] = spread_out(one_hot(WHOLE * CHUNK, REST))
        all_of(brecv.at[l, pl.ds(2, 4)], br.at[l, 2])
        ending.append((brecv.at[l], bs.at[l]))
        own0 = part[pl.ds(pl.multiple_of(CX * x, CD), CD)]
        own1 = part[pl.ds(pl.multiple_of(CX * x + CD, CD), CD)]
        low = own0 + brecv[l, 2].astype(F32) + brecv[l, 5].astype(F32)
        high = own1 + brecv[l, 3].astype(F32) + brecv[l, 4].astype(F32)
        grad = grad + jnp.concatenate([low, high], axis=0) * der[l]

    stem_copies = reduce_y(
        1, jnp.dot(grad.astype(BF16), letters[...], preferred_element_type=F32)
    )
    stem_copies = reduce_z(1, stem_copies)
    y_stage(waiting_y)
    z_stage(waiting_z.pop(0))
    stem_copies = reduce_g(1, stem_copies)
    while waiting_z:
        z_stage(waiting_z.pop(0))
    stem_out[...] = reduce_end(1, stem_copies)

    all_of(gen.at[pl.ds(0, NS - 1)], gsend.at[0])
    all_of(stwo.at[pl.ds(0, NS - 1)], sstwo.at[0])
    for ref, sem in ending:
        all_of(ref, sem)
    for copy in pending:
        copy.wait_send()


def deliver(score, conv, stem, head, score_to, conv_to, stem_to, head_to, sem):
    copies = [
        pltpu.make_async_copy(
            head.at[pl.ds(24 * i, 24)], head_to.at[pl.ds(24 * i, 24)], sem.at[2 + LAYERS + i]
        )
        for i in range(4)
    ]
    for l in range(LAYERS):
        copies.append(pltpu.make_async_copy(conv.at[l], conv_to.at[l], sem.at[2 + l]))
    copies.append(pltpu.make_async_copy(stem, stem_to, sem.at[0]))
    copies.append(pltpu.make_async_copy(score, score_to, sem.at[1]))
    for copy in copies:
        copy.start()
    for copy in copies:
        copy.wait()


def shards(
    genome, stem_weight, dilated_filter_weight, head_weight, window_start, window_track, targets
):
    dma = pltpu.SemaphoreType.DMA
    V = pltpu.VMEM
    scratch = [
        V((NS, T // NS, 128), jnp.int32), V((NS, T // NS, 128), jnp.int32), dma((1,)), dma((1,)),
        V((CD, TRACKS), BF16),
        V((CX, NL), BF16), V((CX, NW), BF16), V((LAYERS, 3, CX, C), BF16),
        dma((2 + LAYERS,)), dma((2 + LAYERS,)), dma((2 + LAYERS,)),
        V((T, NL), BF16),
        V((LAYERS, NX, 2, CD, T), BF16), V((LAYERS, NX, 2, CD, T), BF16),
        V((LAYERS, CX, T), F32), dma((LAYERS,)), dma((LAYERS, 3)),
        dma((LAYERS,)), dma((LAYERS,)),
        V((NC, 1, NW), F32), dma((1,)), dma((1,)),
        V((NS, 1, NW), F32), dma((1,)), dma((1,)),
        V((C, T), F32), V((LAYERS, NX, 2, CD, T), BF16), V((LAYERS, 6, CD, T), BF16),
        V((LAYERS, 2, CD, T), BF16), dma((LAYERS,)), dma((LAYERS, 3)),
        V((LAYERS, CX, T), BF16), V((LAYERS, CD, T), BF16), dma((LAYERS,)), dma((LAYERS,)),
        V((LAYERS, C, KO), BF16), V((LAYERS, NY, CX, KO), BF16),
        dma((LAYERS,)), dma((LAYERS,)),
        V((LAYERS, NZ, CZ, KO), F32), V((LAYERS, NZ, CZ, KO), BF16),
        V((LAYERS, NZ, CZ, KO), BF16), dma((LAYERS,)), dma((LAYERS,)),
        V((2, 2, NY, CD, 128), BF16), V((2, 2 * NY, CD, 128), BF16),
        V((2, NZ, CD, 128), BF16), V((2, NY, CD, 128), F32),
        dma((2,)), dma((2,)), dma((2,)), dma((2,)), dma((2,)), dma((2,)), V((KO, NW), BF16),
    ]
    vm = pl.BlockSpec(memory_space=pltpu.VMEM)
    hbm = pl.BlockSpec(memory_space=pl.ANY)
    score, conv_grad, stem_grad, head_grad = pl.pallas_call(
        tower,
        out_shape=(
            V((1, NW), F32), V((LAYERS, 3, CZ, CD), F32), V((CD, NL), F32), V((CD, TRACKS), F32),
        ),
        in_specs=[vm, hbm, hbm, hbm, vm, vm, vm],
        out_specs=(vm, vm, vm, vm),
        scratch_shapes=scratch,
        compiler_params=pltpu.CompilerParams(
            collective_id=0, has_side_effects=True, vmem_limit_bytes=60 * 1024 * 1024
        ),
    )(
        genome, stem_weight, dilated_filter_weight, head_weight,
        window_start.reshape(1, NW), window_track.reshape(1, NW), targets.reshape(1, NW),
    )
    results = (score, conv_grad, stem_grad, head_grad)
    score, conv_grad, stem_grad, head_grad = pl.pallas_call(
        deliver,
        out_shape=tuple(jax.ShapeDtypeStruct(r.shape, F32) for r in results),
        in_specs=[vm] * 4,
        out_specs=(hbm,) * 4,
        scratch_shapes=[dma((2 + LAYERS + 4,))],
    )(*[pltpu.with_memory_space_constraint(r, pltpu.VMEM) for r in results])
    return (score.reshape(NW), conv_grad.transpose(0, 1, 3, 2), stem_grad, head_grad)


def solution(mesh):
    return jax.shard_map(
        shards,
        mesh=mesh,
        in_specs=(
            P("seq", None),
            P("ch", None),
            P(None, None, "ch", None),
            P("ch", None),
            P(),
            P(),
            P(),
        ),
        out_specs=(P(), P(None, None, "ch", "seq"), P("ch", None), P("ch", None)),
        check_vma=False,
    )
```
